512 devices in a mesh: seq: 32 (over z, x_hi), head: 16 (over x_lo, y, core).
Axes of the slice: x: 4 (x_hi: 2, x_lo: 2; x = x_hi * 2 + x_lo), y: 4, z: 16, core: 2. Of those that a mesh axis runs over, the one named last changes fastest.
Arguments:
- queries: bfloat16 [32768, 4096], P('seq', 'head'), may hold values from -6 to 6
- keys: bfloat16 [32768, 2048], P('seq', 'head'), may hold values from -6 to 6
- values: bfloat16 [32768, 2048], P('seq', 'head'), may hold values from -6 to 6
- grad_out: bfloat16 [32768, 4096], P('seq', 'head'), may hold values from -6 to 6
- starts: int32 [256], P('seq'), may hold values 0 or 1
Outputs:
- grad_queries: bfloat16 [32768, 4096], P('seq', 'head')
- grad_keys: bfloat16 [32768, 2048], P('seq', 'head')
- grad_values: bfloat16 [32768, 2048], P('seq', 'head')
The draws below stay inside these ranges and needn't reach their ends.
Inputs may be any that keep to these rules, and one draw needn't show every extreme that they name: `starts`: blocks of 128 tokens, in storage order.
All inputs are finite; a program needn't handle non-finite values.
Results may differ from the reference program's by a relative error of at most 0.0087.
Values may be sent and summed in bfloat16 or wider, within the bound.
A program may use at most 64 MiB of HBM per device.

```python
import jax
import jax.numpy as jnp
import numpy as np
from jax import lax

HEAD_SIZE = 128
WINDOW = 1024
QUERY_PER_KEY = 2
BLOCK = 128
KEY_VALUE_HEADS = 16
HQ = 32
PIECE_TOKENS = 512
PIECE_COUNT = 64
SEQUENCE_TOKENS = 32768
NBLK = 256
N_SEQ = 32


def draw_queries(key, part):
    return jnp.clip(jax.random.normal(jax.random.fold_in(key, 3), (SEQUENCE_TOKENS, HQ * HEAD_SIZE), jnp.float32), -4.0, 4.0).astype(jnp.bfloat16)


def draw_keys(key, part):
    return jnp.clip(jax.random.normal(jax.random.fold_in(key, 5), (SEQUENCE_TOKENS, KEY_VALUE_HEADS * HEAD_SIZE), jnp.float32), -4.0, 4.0).astype(jnp.bfloat16)


def touch_ends(result, own_key, smallest, high):
    spot = [jax.random.randint(jax.random.fold_in(own_key, axis), (), 0, length) for axis, length in enumerate(result.shape)]
    main_axis = result.shape.index(max(result.shape))
    next_to = spot[:main_axis] + [(spot[main_axis] + 1) % result.shape[main_axis]] + spot[main_axis + 1:]
    return result.at[tuple(spot)].set(smallest).at[tuple(next_to)].set(high)


def block_levels(stream_key, shape, split, least, largest):
    level = 1.0
    for position, shards_of in split:
        heights = jax.random.uniform(jax.random.fold_in(jax.random.fold_in(stream_key, 6), position), (shards_of,), jnp.float32, least / len(split), largest / len(split))
        level = level * jnp.repeat(jnp.exp(heights), shape[position] // shards_of).reshape((-1,) + (1,) * (len(shape) - 1 - position))
    return level


def scatter_about(own_key, shape, deviation, bound, cuts=(), kind=jnp.bfloat16):
    loudness = block_levels(own_key, shape, cuts, -0.22, 0.18) if cuts else 1.0
    values = jax.random.normal(own_key, shape, jnp.float32) * deviation * loudness
    return jnp.minimum(jnp.maximum(values, -bound), bound).astype(kind)


def setup_inputs(seed: int = 0) -> dict:
    splits = jax.random.split(jax.random.key(seed), 6)
    return {
        "queries": draw_queries(jax.random.fold_in(splits[5], 71), 0),
        "keys": draw_keys(jax.random.fold_in(splits[5], 71), 0),
        "values": scatter_about(splits[2], (SEQUENCE_TOKENS, KEY_VALUE_HEADS * HEAD_SIZE), 1.0, 6.0, ((0, 32), (1, 16))),
        "grad_out": scatter_about(splits[3], (SEQUENCE_TOKENS, HQ * HEAD_SIZE), 1.0, 6.0, ((0, 32), (1, 16))),
        "starts": touch_ends((jax.random.randint(splits[4], (NBLK,), 0, 8) < 1).astype(jnp.int32), jax.random.fold_in(splits[4], 1), 0, 1),
    }


query_scaling = 168.0 ** -0.5


def natural_places(n_seq):
    places = []
    for piece in range(2 * n_seq):
        if piece < n_seq:
            places.append(2 * piece)
        else:
            places.append(2 * (2 * n_seq - 1 - piece) + 1)
    return np.array(places, dtype=np.int32)


def reference(queries, keys, values, grad_out, starts):
    storage_lookup = natural_places(N_SEQ)
    inverse_order = np.argsort(storage_lookup).astype(np.int32)
    q_flat = queries.reshape(PIECE_COUNT, PIECE_TOKENS, HQ * HEAD_SIZE)[storage_lookup].reshape(SEQUENCE_TOKENS, HQ * HEAD_SIZE)
    g_flat = grad_out.reshape(PIECE_COUNT, PIECE_TOKENS, HQ * HEAD_SIZE)[storage_lookup].reshape(SEQUENCE_TOKENS, HQ * HEAD_SIZE)
    key_natural_order = keys.reshape(PIECE_COUNT, PIECE_TOKENS, KEY_VALUE_HEADS * HEAD_SIZE)[storage_lookup].reshape(SEQUENCE_TOKENS, KEY_VALUE_HEADS * HEAD_SIZE)
    value_natural_order = values.reshape(PIECE_COUNT, PIECE_TOKENS, KEY_VALUE_HEADS * HEAD_SIZE)[storage_lookup].reshape(SEQUENCE_TOKENS, KEY_VALUE_HEADS * HEAD_SIZE)
    start_nat = starts.reshape(PIECE_COUNT, PIECE_TOKENS // BLOCK)[storage_lookup].reshape(NBLK)
    doc_ids = jnp.cumsum(start_nat).astype(jnp.int32)
    token_doc = jnp.repeat(doc_ids, BLOCK)
    padding_rows = 2 * PIECE_TOKENS
    key_padded_rows = jnp.concatenate([jnp.zeros((padding_rows, KEY_VALUE_HEADS * HEAD_SIZE), keys.dtype), key_natural_order])
    value_padded_rows = jnp.concatenate([jnp.zeros((padding_rows, KEY_VALUE_HEADS * HEAD_SIZE), values.dtype), value_natural_order])
    doc_pad = jnp.concatenate([jnp.full((padding_rows,), -1, jnp.int32), token_doc])

    def one_piece(piece):
        begin = (piece * PIECE_TOKENS).astype(jnp.int32)
        query_rows_local = lax.dynamic_slice_in_dim(q_flat, begin, PIECE_TOKENS, 0)
        gradient_rows = lax.dynamic_slice_in_dim(g_flat, begin, PIECE_TOKENS, 0)
        key_rows_local = lax.dynamic_slice_in_dim(key_padded_rows, begin, 3 * PIECE_TOKENS, 0)
        value_rows_local = lax.dynamic_slice_in_dim(value_padded_rows, begin, 3 * PIECE_TOKENS, 0)
        d_rows = lax.dynamic_slice_in_dim(doc_pad, begin, 3 * PIECE_TOKENS, 0)
        key_pos = begin - 2 * PIECE_TOKENS + jnp.arange(3 * PIECE_TOKENS, dtype=jnp.int32)
        query_pos = begin + jnp.arange(PIECE_TOKENS, dtype=jnp.int32)
        offset = query_pos[:, None] - key_pos[None, :]
        query_doc = d_rows[2 * PIECE_TOKENS:]
        allowed = (offset >= 0) & (offset < WINDOW) & (key_pos[None, :] >= 0) & (query_doc[:, None] == d_rows[None, :])
        query_float = query_rows_local.astype(jnp.float32).reshape(PIECE_TOKENS, KEY_VALUE_HEADS, QUERY_PER_KEY, HEAD_SIZE)
        gradient_float = gradient_rows.astype(jnp.float32).reshape(PIECE_TOKENS, KEY_VALUE_HEADS, QUERY_PER_KEY, HEAD_SIZE)
        key_float = key_rows_local.astype(jnp.float32).reshape(3 * PIECE_TOKENS, KEY_VALUE_HEADS, HEAD_SIZE)
        value_float = value_rows_local.astype(jnp.float32).reshape(3 * PIECE_TOKENS, KEY_VALUE_HEADS, HEAD_SIZE)
        scores = jnp.einsum("qhgd,khd->hgqk", query_float, key_float) * query_scaling
        masked = jnp.where(allowed, scores, -jnp.inf)
        row_max = jnp.max(masked, axis=3, keepdims=True)
        exp_terms = jnp.where(allowed, jnp.exp(scores - row_max), 0.0)
        weights = exp_terms / jnp.sum(exp_terms, axis=3, keepdims=True)
        weights_bfloat = lax.optimization_barrier(weights.astype(jnp.bfloat16)).astype(jnp.float32)
        dweights = jnp.einsum("qhgd,khd->hgqk", gradient_float, value_float)
        row_dot = jnp.sum(weights * dweights, axis=3, keepdims=True)
        score_gradient = lax.optimization_barrier((weights * (dweights - row_dot)).astype(jnp.bfloat16)).astype(jnp.float32)
        grad_q = (jnp.einsum("hgqk,khd->qhgd", score_gradient, key_float) * query_scaling).reshape(PIECE_TOKENS, HQ * HEAD_SIZE).astype(jnp.bfloat16)
        key_gradient = (jnp.einsum("wyjx,jwyo->xwo", score_gradient, query_float) * query_scaling).reshape(3 * PIECE_TOKENS, KEY_VALUE_HEADS * HEAD_SIZE)
        value_gradient = jnp.einsum("wyjx,jwyo->xwo", weights_bfloat, gradient_float).reshape(3 * PIECE_TOKENS, KEY_VALUE_HEADS * HEAD_SIZE)
        return grad_q, key_gradient, value_gradient

    dq_nat, dk_terms, dv_terms = lax.map(one_piece, jnp.arange(PIECE_COUNT, dtype=jnp.int32))

    def combine(gradient_terms):
        split_rows = gradient_terms.reshape(PIECE_COUNT, 3, PIECE_TOKENS, KEY_VALUE_HEADS * HEAD_SIZE)
        empty_zero_rows = jnp.zeros((2, PIECE_TOKENS, KEY_VALUE_HEADS * HEAD_SIZE), split_rows.dtype)
        older_piece = jnp.concatenate([split_rows[2:, 0], empty_zero_rows])
        nearer_piece = jnp.concatenate([split_rows[1:, 1], empty_zero_rows[:1]])
        return (split_rows[:, 2] + nearer_piece + older_piece)[inverse_order].reshape(SEQUENCE_TOKENS, KEY_VALUE_HEADS * HEAD_SIZE).astype(jnp.bfloat16)

    grad_queries = dq_nat[inverse_order].reshape(SEQUENCE_TOKENS, HQ * HEAD_SIZE)
    return grad_queries, combine(dk_terms), combine(dv_terms)
```

```python
import functools

import jax
import jax.numpy as jnp
from jax import lax
from jax.experimental import pallas as pl
from jax.experimental.pallas import tpu as pltpu
from jax.sharding import PartitionSpec as P

HEAD_SIZE = 128
BLOCK = 128
PIECE = 512
BLOCKS = PIECE // BLOCK
HEADS = 2
TILE = HEADS * BLOCK
LANES = BLOCKS * TILE
OWN, NEAR, FAR = 0, 1, 2
MASKED = -1e30
MESH = pl.DeviceIdType.MESH

query_scaling = 168.0 ** (-0.5)
exp2_scaling = query_scaling * 1.4426950408889634


def span(chunk, i):
    if chunk == OWN:
        return range(i + 1)
    if chunk == FAR:
        return range(i, BLOCKS)
    return range(BLOCKS)


def rows_of(j):
    return slice(j * BLOCK, (j + 1) * BLOCK)


def lanes_of(i):
    return slice(i * TILE, (i + 1) * TILE)


def last_dims(a, b):
    return lax.dot_general(a, b, (((1,), (1,)), ((), ())), preferred_element_type=jnp.float32)


def kernel(
    n, q_hbm, g_hbm, k_hbm, v_hbm, starts, dq_hbm, dk_hbm, dv_hbm,
    q_in, g_in, k_all, v_all, k_t, table, tables, q_cat, g_cat, terms, dweights, dscores, stats,
    grads_out, grads_in, grads_own, dq_out, dk_out, dv_out,
    load_sem, store_sem, k_send, v_send, t_send, k_recv, v_recv, t_recv, g_send, g_recv,
):
    s = lax.axis_index("seq")
    head = lax.axis_index("head")

    loads = [
        pltpu.make_async_copy(q_hbm, q_in, load_sem.at[0]),
        pltpu.make_async_copy(g_hbm, g_in, load_sem.at[1]),
    ]
    for half in range(2):
        piece = pl.ds(half * PIECE, PIECE)
        loads.append(pltpu.make_async_copy(k_hbm.at[piece], k_all.at[half, OWN], load_sem.at[2 + 2 * half]))
        loads.append(pltpu.make_async_copy(v_hbm.at[piece], v_all.at[half, OWN], load_sem.at[3 + 2 * half]))
    for copy in loads:
        copy.start()

    barrier = pltpu.get_barrier_semaphore()
    for step in (-2, -1, 1, 2):
        there = s + step

        @pl.when((there >= 0) & (there < n))
        def _():
            pl.semaphore_signal(barrier, inc=1, device_id=(there, head), device_id_type=MESH)

    for half in range(2):
        own = [starts[half * BLOCKS + j].astype(jnp.float32) for j in range(BLOCKS)]
        line = lax.broadcasted_iota(jnp.int32, (8, BLOCK), 0)
        after = jnp.zeros((8, BLOCK), jnp.float32)
        for j in range(BLOCKS):
            after = after + jnp.where((line < j) | (line == BLOCKS), own[j], 0.0)
        table[half] = after

    @pl.when(s == 0)
    def _():
        k_all[0, NEAR] = jnp.zeros((PIECE, HEAD_SIZE), jnp.bfloat16)
        v_all[0, NEAR] = jnp.zeros((PIECE, HEAD_SIZE), jnp.bfloat16)
        tables[0, NEAR] = jnp.ones((8, BLOCK), jnp.float32)
        grads_in[1, NEAR] = jnp.zeros((PIECE, 2 * HEAD_SIZE), jnp.bfloat16)

    @pl.when(s <= 1)
    def _():
        k_all[0, FAR] = jnp.zeros((PIECE, HEAD_SIZE), jnp.bfloat16)
        v_all[0, FAR] = jnp.zeros((PIECE, HEAD_SIZE), jnp.bfloat16)
        tables[0, FAR] = jnp.ones((8, BLOCK), jnp.float32)
        grads_in[1, FAR] = jnp.zeros((PIECE, 2 * HEAD_SIZE), jnp.bfloat16)

    pl.semaphore_wait(barrier, jnp.minimum(s, 2) + jnp.minimum(n - 1 - s, 2))

    folded = s > n - 3
    beyond = jnp.where(folded, 2 * n - 3 - s, s + 2)
    other_half = jnp.where(folded, 1, 0)
    same_half = jnp.where(folded, 0, 1)

    def pass_piece(half, slot, there, to_half):
        piece = pl.ds(half * PIECE, PIECE)
        target = dict(device_id=(there, head), device_id_type=MESH)
        at = (half, slot - 1)
        to = (to_half, slot - 1)
        return [
            pltpu.make_async_remote_copy(
                table.at[half], tables.at[to_half, slot], t_send.at[at], t_recv.at[to], **target),
            pltpu.make_async_remote_copy(
                k_hbm.at[piece], k_all.at[to_half, slot], k_send.at[at], k_recv.at[to], **target),
            pltpu.make_async_remote_copy(
                v_hbm.at[piece], v_all.at[to_half, slot], v_send.at[at], v_recv.at[to], **target),
        ]

    def pass_grads(half, slot, there, to_half):
        return pltpu.make_async_remote_copy(
            grads_out.at[half, slot - 1], grads_in.at[to_half, slot], g_send.at[half, slot - 1],
            g_recv.at[to_half, slot - 1], device_id=(there, head), device_id_type=MESH)

    at_fold = s == n - 1
    forward = [
        (s < n - 1, lambda: pass_piece(0, NEAR, s + 1, 0)),
        (s >= 1, lambda: pass_piece(1, NEAR, s - 1, 1)),
        (s >= 0, lambda: pass_piece(0, FAR, beyond, other_half)),
        (s >= 2, lambda: pass_piece(1, FAR, s - 2, 1)),
    ]
    across = [
        pltpu.make_async_copy(table.at[0], tables.at[1, NEAR], t_recv.at[1, 0]),
        pltpu.make_async_copy(k_hbm.at[pl.ds(0, PIECE)], k_all.at[1, NEAR], k_recv.at[1, 0]),
        pltpu.make_async_copy(v_hbm.at[pl.ds(0, PIECE)], v_all.at[1, NEAR], v_recv.at[1, 0]),
    ]
    for wanted, copies in forward:

        @pl.when(wanted)
        def _():
            for copy in copies():
                copy.start()

    @pl.when(at_fold)
    def _():
        for copy in across:
            copy.start()

    for copy in loads:
        copy.wait()

    for half in range(2):
        for i in range(BLOCKS):
            for h in range(HEADS):
                rows = slice(half * PIECE + i * BLOCK, half * PIECE + (i + 1) * BLOCK)
                to = slice(i * TILE + h * BLOCK, i * TILE + (h + 1) * BLOCK)
                cols = slice(h * HEAD_SIZE, (h + 1) * HEAD_SIZE)
                q_cat[half, to, :] = q_in[rows, cols]
                g_cat[half, to, :] = g_in[rows, cols]

    key_row = lax.broadcasted_iota(jnp.int32, (BLOCK, TILE), 0)
    query_row = lax.broadcasted_iota(jnp.int32, (BLOCK, TILE), 1) % BLOCK
    causal = key_row <= query_row

    def first_pass(half, chunk):
        k_t[half, chunk] = k_all[half, chunk].T
        for i in range(BLOCKS):
            begun = [starts[half * BLOCKS + j] for j in range(BLOCKS)]
            q_i = q_cat[half, lanes_of(i), :]
            g_i = g_cat[half, lanes_of(i), :]
            scores = []
            for j in span(chunk, i):
                x = last_dims(k_all[half, chunk, rows_of(j), :], q_i) * exp2_scaling
                if chunk == OWN:
                    count = functools.reduce(lambda a, b: a + b, begun[j + 1 : i + 1], jnp.int32(0))
                    since = jnp.full((1, BLOCK), count.astype(jnp.float32))
                else:
                    count = functools.reduce(lambda a, b: a + b, begun[: i + 1])
                    since = tables[half, chunk, j : j + 1, :] + count.astype(jnp.float32)
                    if chunk == FAR:
                        since = since + tables[half, NEAR, BLOCKS : BLOCKS + 1, :]
                if not (chunk == OWN and j == i):
                    bias = jnp.where(since > 0.5, MASKED, 0.0)
                    x = x + jnp.concatenate([bias, bias], axis=1)
                if chunk == OWN and j == i:
                    x = jnp.where(causal, x, MASKED)
                if chunk == FAR and j == i:
                    x = jnp.where(causal, MASKED, x)
                scores.append(x)
            top = functools.reduce(jnp.maximum, [jnp.max(x, axis=0, keepdims=True) for x in scores])
            total = jnp.zeros((1, TILE), jnp.float32)
            dotted = jnp.zeros((1, TILE), jnp.float32)
            for j, x in zip(span(chunk, i), scores):
                e = jnp.exp2(x - top)
                w = last_dims(v_all[half, chunk, rows_of(j), :], g_i)
                total = total + jnp.sum(e, axis=0, keepdims=True)
                dotted = dotted + jnp.sum(e * w, axis=0, keepdims=True)
                terms[half, chunk, rows_of(j), lanes_of(i)] = e
                dweights[half, chunk, rows_of(j), lanes_of(i)] = w
            stats[half, chunk, 0:1, lanes_of(i)] = top
            stats[half, chunk, 1:2, lanes_of(i)] = total
            stats[half, chunk, 2:3, lanes_of(i)] = dotted

    def merge(half):
        tops = [stats[half, c, 0:1, :] for c in range(3)]
        top = functools.reduce(jnp.maximum, tops)
        ratios = [jnp.exp2(t - top) for t in tops]
        total = sum(stats[half, c, 1:2, :] * ratios[c] for c in range(3))
        dotted = sum(stats[half, c, 2:3, :] * ratios[c] for c in range(3))
        inverse = 1.0 / total
        for c in range(3):
            stats[half, c, 3:4, :] = ratios[c] * inverse
        stats[half, OWN, 4:5, :] = dotted * inverse

    def second_pass(half, chunk):
        for j in range(BLOCKS):
            dk = jnp.zeros((BLOCK, HEAD_SIZE), jnp.float32)
            dv = jnp.zeros((BLOCK, HEAD_SIZE), jnp.float32)
            for i in range(BLOCKS):
                if j not in span(chunk, i):
                    continue
                p = terms[half, chunk, rows_of(j), lanes_of(i)] * stats[half, chunk, 3:4, lanes_of(i)]
                d = p * (dweights[half, chunk, rows_of(j), lanes_of(i)] - stats[half, OWN, 4:5, lanes_of(i)])
                d = d.astype(jnp.bfloat16)
                dscores[half, chunk, rows_of(j), lanes_of(i)] = d
                dk = dk + jnp.dot(d, q_cat[half, lanes_of(i), :], preferred_element_type=jnp.float32)
                dv = dv + jnp.dot(
                    p.astype(jnp.bfloat16), g_cat[half, lanes_of(i), :], preferred_element_type=jnp.float32)
            both = jnp.concatenate([dk * query_scaling, dv], axis=1)
            if chunk == OWN:
                grads_own[half, rows_of(j), :] = both
            else:
                grads_out[half, chunk - 1, rows_of(j), :] = both.astype(jnp.bfloat16)

    def query_pass(half):
        for i in range(BLOCKS):
            total = jnp.zeros((HEAD_SIZE, TILE), jnp.float32)
            for c in range(3):
                js = span(c, i)
                keys = slice(js[0] * BLOCK, (js[-1] + 1) * BLOCK)
                total = total + jnp.dot(
                    k_t[half, c, :, keys], dscores[half, c, keys, lanes_of(i)], preferred_element_type=jnp.float32)
            turned = (total * query_scaling).T.astype(jnp.bfloat16)
            rows = pl.ds(half * PIECE + i * BLOCK, BLOCK)
            for h in range(HEADS):
                dq_out[rows, h * HEAD_SIZE : (h + 1) * HEAD_SIZE] = turned[h * BLOCK : (h + 1) * BLOCK, :]

    def await_piece(half, slot):
        pltpu.make_async_copy(table.at[0], tables.at[half, slot], t_recv.at[half, slot - 1]).wait()
        pltpu.make_async_copy(k_hbm.at[pl.ds(0, PIECE)], k_all.at[half, slot], k_recv.at[half, slot - 1]).wait()
        pltpu.make_async_copy(v_hbm.at[pl.ds(0, PIECE)], v_all.at[half, slot], v_recv.at[half, slot - 1]).wait()

    def await_grads(half, slot):
        pltpu.make_async_copy(grads_out.at[0, 0], grads_in.at[half, slot], g_recv.at[half, slot - 1]).wait()

    for half in range(2):
        first_pass(half, OWN)

    backward = [
        [(s >= 1, lambda: pass_grads(0, NEAR, s - 1, 0)), (s >= 2, lambda: pass_grads(0, FAR, s - 2, 0))],
        [(s < n - 1, lambda: pass_grads(1, NEAR, s + 1, 1)), (s >= 0, lambda: pass_grads(1, FAR, beyond, same_half))],
    ]
    home = pltpu.make_async_copy(grads_out.at[1, 0], grads_in.at[0, NEAR], g_recv.at[0, 0])

    for half in range(2):
        for slot in (NEAR, FAR):
            if half == 1:
                await_piece(half, slot)
            else:

                @pl.when(s >= slot)
                def _():
                    await_piece(half, slot)

            first_pass(half, slot)
        merge(half)
        for slot in (NEAR, FAR):
            second_pass(half, slot)
            wanted, copy = backward[half][slot - 1]

            @pl.when(wanted)
            def _():
                copy().start()

            if half == 1 and slot == NEAR:

                @pl.when(at_fold)
                def _():
                    home.start()

    stores = []
    for half in range(2):
        second_pass(half, OWN)
        query_pass(half)
    stores.append(pltpu.make_async_copy(dq_out, dq_hbm, store_sem.at[0]))
    stores[0].start()

    for half in range(2):
        for slot in (NEAR, FAR):
            if half == 0:
                await_grads(half, slot)
            else:

                @pl.when(s >= slot)
                def _():
                    await_grads(half, slot)

        total = (
            grads_own[half]
            + grads_in[half, NEAR].astype(jnp.float32)
            + grads_in[half, FAR].astype(jnp.float32)
        ).astype(jnp.bfloat16)
        piece = pl.ds(half * PIECE, PIECE)
        dk_out[piece, :] = total[:, :HEAD_SIZE]
        dv_out[piece, :] = total[:, HEAD_SIZE:]
        for which, (made, to) in enumerate(((dk_out, dk_hbm), (dv_out, dv_hbm))):
            copy = pltpu.make_async_copy(made.at[piece], to.at[piece], store_sem.at[1 + 2 * half + which])
            copy.start()
            stores.append(copy)

    for wanted, copies in forward:

        @pl.when(wanted)
        def _():
            for copy in copies():
                copy.wait_send()

    for half in range(2):
        for wanted, copy in backward[half]:

            @pl.when(wanted)
            def _():
                copy().wait_send()

    for copy in stores:
        copy.wait()


def on_device(queries, keys, values, grad_out, starts):
    n = lax.axis_size("seq")
    bf16, f32 = jnp.bfloat16, jnp.float32
    vmem, dma = pltpu.VMEM, pltpu.SemaphoreType.DMA
    anywhere = pl.BlockSpec(memory_space=pl.ANY)
    return pl.pallas_call(
        functools.partial(kernel, n),
        out_shape=(
            jax.ShapeDtypeStruct(queries.shape, bf16),
            jax.ShapeDtypeStruct(keys.shape, bf16),
            jax.ShapeDtypeStruct(values.shape, bf16),
        ),
        in_specs=[anywhere] * 4 + [pl.BlockSpec(memory_space=pltpu.SMEM)],
        out_specs=(anywhere,) * 3,
        scratch_shapes=[
            vmem((2 * PIECE, 2 * HEAD_SIZE), bf16),
            vmem((2 * PIECE, 2 * HEAD_SIZE), bf16),
            vmem((2, 3, PIECE, HEAD_SIZE), bf16),
            vmem((2, 3, PIECE, HEAD_SIZE), bf16),
            vmem((2, 3, HEAD_SIZE, PIECE), bf16),
            vmem((2, 8, BLOCK), f32),
            vmem((2, 3, 8, BLOCK), f32),
            vmem((2, LANES, HEAD_SIZE), bf16),
            vmem((2, LANES, HEAD_SIZE), bf16),
            vmem((2, 3, PIECE, LANES), f32),
            vmem((2, 3, PIECE, LANES), f32),
            vmem((2, 3, PIECE, LANES), bf16),
            vmem((2, 3, 8, LANES), f32),
            vmem((2, 2, PIECE, 2 * HEAD_SIZE), bf16),
            vmem((2, 3, PIECE, 2 * HEAD_SIZE), bf16),
            vmem((2, PIECE, 2 * HEAD_SIZE), f32),
            vmem((2 * PIECE, 2 * HEAD_SIZE), bf16),
            vmem((2 * PIECE, HEAD_SIZE), bf16),
            vmem((2 * PIECE, HEAD_SIZE), bf16),
            dma((6,)),
            dma((5,)),
        ]
        + [dma((2, 2))] * 8,
        compiler_params=pltpu.CompilerParams(
            collective_id=0, has_side_effects=True, vmem_limit_bytes=58 << 20
        ),
    )(queries, grad_out, keys, values, starts)


def solution(mesh):
    in_specs = (P("seq", "head"), P("seq", "head"), P("seq", "head"), P("seq", "head"), P("seq"))
    out_specs = (P("seq", "head"), P("seq", "head"), P("seq", "head"))
    return jax.shard_map(
        on_device, mesh=mesh, in_specs=in_specs, out_specs=out_specs, check_vma=False
    )
```

```python
import functools

import jax
import jax.numpy as jnp
from jax import lax
from jax.experimental import pallas as pl
from jax.experimental.pallas import tpu as pltpu
from jax.sharding import PartitionSpec as P

HEAD_SIZE = 128
BLOCK = 128
PIECE = 512
BLOCKS = PIECE // BLOCK
HEADS = 2
TILE = HEADS * BLOCK
LANES = BLOCKS * TILE
OWN, NEAR, FAR = 0, 1, 2
MASKED = -1e30
MESH = pl.DeviceIdType.MESH

query_scaling = 168.0 ** (-0.5)
exp2_scaling = query_scaling * 1.4426950408889634


def span(chunk, i):
    if chunk == OWN:
        return range(i + 1)
    if chunk == FAR:
        return range(i, BLOCKS)
    return range(BLOCKS)


def rows_of(j):
    return slice(j * BLOCK, (j + 1) * BLOCK)


def lanes_of(i):
    return slice(i * TILE, (i + 1) * TILE)


def last_dims(a, b):
    return lax.dot_general(a, b, (((1,), (1,)), ((), ())), preferred_element_type=jnp.float32)


def kernel(
    n, q_hbm, g_hbm, k_hbm, v_hbm, starts, dq_hbm, dk_hbm, dv_hbm,
    q_in, g_in, k_all, v_all, k_t, table, tables, k_hop, q_cat, g_cat, terms, dweights, dscores, stats,
    grads_out, grads_in, grads_own, dq_out, dk_out, dv_out,
    load_sem, store_sem, k_send, v_send, t_send, k_recv, v_recv, t_recv, g_send, g_recv,
):
    s = lax.axis_index("seq")
    head = lax.axis_index("head")

    loads = [
        pltpu.make_async_copy(q_hbm, q_in, load_sem.at[0]),
        pltpu.make_async_copy(g_hbm, g_in, load_sem.at[1]),
    ]
    for half in range(2):
        piece = pl.ds(half * PIECE, PIECE)
        loads.append(pltpu.make_async_copy(k_hbm.at[piece], k_all.at[half, OWN], load_sem.at[2 + 2 * half]))
        loads.append(pltpu.make_async_copy(v_hbm.at[piece], v_all.at[half, OWN], load_sem.at[3 + 2 * half]))
    for copy in loads:
        copy.start()

    barrier = pltpu.get_barrier_semaphore()
    for step in (-2, -1, 1, 2):
        there = s + step

        @pl.when((there >= 0) & (there < n))
        def _():
            pl.semaphore_signal(barrier, inc=1, device_id=(there, head), device_id_type=MESH)

    for half in range(2):
        own = [starts[half * BLOCKS + j].astype(jnp.float32) for j in range(BLOCKS)]
        line = lax.broadcasted_iota(jnp.int32, (8, BLOCK), 0)
        after = jnp.zeros((8, BLOCK), jnp.float32)
        for j in range(BLOCKS):
            after = after + jnp.where((line < j) | (line == BLOCKS), own[j], 0.0)
        table[half] = after

    @pl.when(s == n - 2)
    def _():
        grads_in[0, FAR] = jnp.zeros((PIECE, 2 * HEAD_SIZE), jnp.bfloat16)

    @pl.when(s == 0)
    def _():
        k_all[0, NEAR] = jnp.zeros((PIECE, HEAD_SIZE), jnp.bfloat16)
        v_all[0, NEAR] = jnp.zeros((PIECE, HEAD_SIZE), jnp.bfloat16)
        tables[0, NEAR] = jnp.ones((8, BLOCK), jnp.float32)
        grads_in[1, NEAR] = jnp.zeros((PIECE, 2 * HEAD_SIZE), jnp.bfloat16)

    @pl.when(s <= 1)
    def _():
        k_all[0, FAR] = jnp.zeros((PIECE, HEAD_SIZE), jnp.bfloat16)
        v_all[0, FAR] = jnp.zeros((PIECE, HEAD_SIZE), jnp.bfloat16)
        tables[0, FAR] = jnp.ones((8, BLOCK), jnp.float32)
        grads_in[1, FAR] = jnp.zeros((PIECE, 2 * HEAD_SIZE), jnp.bfloat16)

    pl.semaphore_wait(barrier, jnp.minimum(s, 2) + jnp.minimum(n - 1 - s, 2))

    folded = s > n - 3
    beyond = jnp.where(folded, 2 * n - 3 - s, s + 2)
    at_fold = s == n - 1
    odd = s % 2 == 1
    first = jnp.where(odd, 0, 1)

    def send_piece(sources, sinks, sends, recvs, there):
        return [
            pltpu.make_async_remote_copy(*refs, device_id=(there, head), device_id_type=MESH)
            for refs in zip(sources, sinks, sends, recvs)
        ]

    def at(refs, *index):
        return [ref.at[index] for ref in refs]

    pieces, sends, recvs = (tables, k_all, v_all), (t_send, k_send, v_send), (t_recv, k_recv, v_recv)

    def own_refs(half):
        piece = pl.ds(half * PIECE, PIECE)
        return table.at[half], k_hbm.at[piece], v_hbm.at[piece]

    def own_piece(half, slot, there):
        return send_piece(
            own_refs(half), at(pieces, half, slot), at(sends, half, slot - 1), at(recvs, half, slot - 1), there)

    def held_piece(half, there):
        return send_piece(
            at(pieces, half, FAR), at(pieces, half, NEAR), at(sends, 2, 0), at(recvs, half, NEAR - 1), there)

    def sidestep():
        return pltpu.make_async_remote_copy(
            own_refs(0)[1], k_hop, k_send.at[2, 1], k_recv.at[2, 0],
            device_id=(n - 4, head), device_id_type=MESH)

    def onward():
        return pltpu.make_async_remote_copy(
            k_hop, k_all.at[0, NEAR], k_send.at[2, 1], k_recv.at[0, NEAR - 1],
            device_id=(n - 2, head), device_id_type=MESH)

    def folded_piece():
        return send_piece(
            own_refs(0), at(pieces, 1, FAR), at(sends, 0, FAR - 1), at(recvs, 1, FAR - 1), n - 2)

    def pass_grads(half, slot, there, to_half):
        return pltpu.make_async_remote_copy(
            grads_out.at[half, slot - 1], grads_in.at[to_half, slot], g_send.at[half, slot - 1],
            g_recv.at[to_half, slot - 1], device_id=(there, head), device_id_type=MESH)

    forward = [
        (~odd, lambda: own_piece(0, NEAR, s + 1)),
        (odd, lambda: own_piece(1, NEAR, s - 1)),
        (at_fold, folded_piece),
        (s == n - 3, lambda: [sidestep()]),
        (s <= n - 3, lambda: own_piece(0, FAR, s + 2)),
        (s >= 2, lambda: own_piece(1, FAR, s - 2)),
    ]
    relays = jnp.where(odd, s >= 3, s <= n - 4)
    relay = lambda: held_piece(jnp.where(odd, 0, 1), jnp.where(odd, s - 1, s + 1))
    across = [
        pltpu.make_async_copy(table.at[0], tables.at[1, NEAR], t_recv.at[1, 0]),
        pltpu.make_async_copy(k_hbm.at[pl.ds(0, PIECE)], k_all.at[1, NEAR], k_recv.at[1, 0]),
        pltpu.make_async_copy(v_hbm.at[pl.ds(0, PIECE)], v_all.at[1, NEAR], v_recv.at[1, 0]),
    ]
    again = [
        pltpu.make_async_copy(kept.at[0, NEAR], kept.at[1, FAR], sem.at[1, 1])
        for kept, sem in ((tables, t_recv), (k_all, k_recv), (v_all, v_recv))
    ]
    for wanted, copies in forward:

        @pl.when(wanted)
        def _():
            for copy in copies():
                copy.start()

    @pl.when(at_fold)
    def _():
        for copy in across:
            copy.start()

    for copy in loads:
        copy.wait()

    for half in range(2):
        for i in range(BLOCKS):
            for h in range(HEADS):
                rows = slice(half * PIECE + i * BLOCK, half * PIECE + (i + 1) * BLOCK)
                to = slice(i * TILE + h * BLOCK, i * TILE + (h + 1) * BLOCK)
                cols = slice(h * HEAD_SIZE, (h + 1) * HEAD_SIZE)
                q_cat[half, to, :] = q_in[rows, cols]
                g_cat[half, to, :] = g_in[rows, cols]

    key_row = lax.broadcasted_iota(jnp.int32, (BLOCK, TILE), 0)
    query_row = lax.broadcasted_iota(jnp.int32, (BLOCK, TILE), 1) % BLOCK
    causal = key_row <= query_row

    def first_pass(half, chunk):
        k_t[half, chunk] = k_all[half, chunk].T
        for i in range(BLOCKS):
            begun = [starts[half * BLOCKS + j] for j in range(BLOCKS)]
            q_i = q_cat[half, lanes_of(i), :]
            g_i = g_cat[half, lanes_of(i), :]
            scores = []
            for j in span(chunk, i):
                x = last_dims(k_all[half, chunk, rows_of(j), :], q_i) * exp2_scaling
                if chunk == OWN:
                    count = functools.reduce(lambda a, b: a + b, begun[j + 1 : i + 1], jnp.int32(0))
                    since = jnp.full((1, BLOCK), count.astype(jnp.float32))
                else:
                    count = functools.reduce(lambda a, b: a + b, begun[: i + 1])
                    since = tables[half, chunk, j : j + 1, :] + count.astype(jnp.float32)
                    if chunk == FAR:
                        since = since + tables[half, NEAR, BLOCKS : BLOCKS + 1, :]
                if not (chunk == OWN and j == i):
                    bias = jnp.where(since > 0.5, MASKED, 0.0)
                    x = x + jnp.concatenate([bias, bias], axis=1)
                if chunk == OWN and j == i:
                    x = jnp.where(causal, x, MASKED)
                if chunk == FAR and j == i:
                    x = jnp.where(causal, MASKED, x)
                scores.append(x)
            top = functools.reduce(jnp.maximum, [jnp.max(x, axis=0, keepdims=True) for x in scores])
            total = jnp.zeros((1, TILE), jnp.float32)
            dotted = jnp.zeros((1, TILE), jnp.float32)
            for j, x in zip(span(chunk, i), scores):
                e = jnp.exp2(x - top)
                w = last_dims(v_all[half, chunk, rows_of(j), :], g_i)
                total = total + jnp.sum(e, axis=0, keepdims=True)
                dotted = dotted + jnp.sum(e * w, axis=0, keepdims=True)
                terms[half, chunk, rows_of(j), lanes_of(i)] = e
                dweights[half, chunk, rows_of(j), lanes_of(i)] = w
            stats[half, chunk, 0:1, lanes_of(i)] = top
            stats[half, chunk, 1:2, lanes_of(i)] = total
            stats[half, chunk, 2:3, lanes_of(i)] = dotted

    def merge(half):
        tops = [stats[half, c, 0:1, :] for c in range(3)]
        top = functools.reduce(jnp.maximum, tops)
        ratios = [jnp.exp2(t - top) for t in tops]
        total = sum(stats[half, c, 1:2, :] * ratios[c] for c in range(3))
        dotted = sum(stats[half, c, 2:3, :] * ratios[c] for c in range(3))
        inverse = 1.0 / total
        for c in range(3):
            stats[half, c, 3:4, :] = ratios[c] * inverse
        stats[half, OWN, 4:5, :] = dotted * inverse

    def second_pass(half, chunk):
        for j in range(BLOCKS):
            dk = jnp.zeros((BLOCK, HEAD_SIZE), jnp.float32)
            dv = jnp.zeros((BLOCK, HEAD_SIZE), jnp.float32)
            for i in range(BLOCKS):
                if j not in span(chunk, i):
                    continue
                p = terms[half, chunk, rows_of(j), lanes_of(i)] * stats[half, chunk, 3:4, lanes_of(i)]
                d = p * (dweights[half, chunk, rows_of(j), lanes_of(i)] - stats[half, OWN, 4:5, lanes_of(i)])
                d = d.astype(jnp.bfloat16)
                dscores[half, chunk, rows_of(j), lanes_of(i)] = d
                dk = dk + jnp.dot(d, q_cat[half, lanes_of(i), :], preferred_element_type=jnp.float32)
                dv = dv + jnp.dot(
                    p.astype(jnp.bfloat16), g_cat[half, lanes_of(i), :], preferred_element_type=jnp.float32)
            both = jnp.concatenate([dk * query_scaling, dv], axis=1)
            if chunk == OWN:
                grads_own[half, rows_of(j), :] = both
            else:
                grads_out[half, chunk - 1, rows_of(j), :] = both.astype(jnp.bfloat16)

    def query_pass(half):
        for i in range(BLOCKS):
            total = jnp.zeros((HEAD_SIZE, TILE), jnp.float32)
            for c in range(3):
                js = span(c, i)
                keys = slice(js[0] * BLOCK, (js[-1] + 1) * BLOCK)
                total = total + jnp.dot(
                    k_t[half, c, :, keys], dscores[half, c, keys, lanes_of(i)], preferred_element_type=jnp.float32)
            turned = (total * query_scaling).T.astype(jnp.bfloat16)
            rows = pl.ds(half * PIECE + i * BLOCK, BLOCK)
            for h in range(HEADS):
                dq_out[rows, h * HEAD_SIZE : (h + 1) * HEAD_SIZE] = turned[h * BLOCK : (h + 1) * BLOCK, :]

    def await_piece(half, slot):
        return [
            pltpu.make_async_copy(*refs)
            for refs in zip(own_refs(0), at(pieces, half, slot), at(recvs, half, slot - 1))
        ]

    def await_grads(half, slot):
        pltpu.make_async_copy(grads_out.at[0, 0], grads_in.at[half, slot], g_recv.at[half, slot - 1]).wait()

    def near_grads(half):
        return pass_grads(half, NEAR, jnp.where(half == 0, s - 1, s + 1), half)

    def far_grads(half):
        there = jnp.where(half == 0, s - 2, beyond)
        return pass_grads(half, FAR, there, jnp.where((half == 0) | folded, 0, 1))

    def near_wanted(half):
        return jnp.where(half == 0, s >= 1, s < n - 1)

    def far_wanted(half):
        return jnp.where(half == 0, s >= 2, s < n - 1)

    home = pltpu.make_async_copy(grads_out.at[1, 0], grads_in.at[0, NEAR], g_recv.at[0, 0])

    for half in range(2):
        first_pass(half, OWN)

    def earlier_pieces(turn, carry):
        half = jnp.where(turn == 0, first, 1 - first)

        @pl.when((half == 1) | (s >= 2))
        def _():
            for which, (awaited, copy) in enumerate(zip(await_piece(half, FAR), relay())):
                awaited.wait()
                able = relays & ~at_fold if which == 1 else relays

                @pl.when(able & (turn == 0))
                def _():
                    copy.start()

        @pl.when((s == n - 4) & (turn == 0))
        def _():
            pltpu.make_async_copy(own_refs(0)[1], k_hop, k_recv.at[2, 0]).wait()
            onward().start()

        @pl.when((half == 1) | (s >= 1))
        def _():
            await_piece(half, NEAR)[0].wait()

        first_pass(half, FAR)

        @pl.when((half == 1) | (s >= 1))
        def _():
            for copy in await_piece(half, NEAR)[1:]:
                copy.wait()

        @pl.when(at_fold & (turn == 0))
        def _():
            for copy in again:
                copy.start()

        first_pass(half, NEAR)
        merge(half)
        second_pass(half, NEAR)

        @pl.when(near_wanted(half) & ~(at_fold & (half == 0)))
        def _():
            near_grads(half).start()

        @pl.when(at_fold & (half == 1))
        def _():
            home.start()

        second_pass(half, FAR)

        @pl.when(far_wanted(half))
        def _():
            far_grads(half).start()

        @pl.when(at_fold & (half == 1))
        def _():
            both = grads_out[0, NEAR - 1].astype(jnp.float32) + grads_out[1, FAR - 1].astype(jnp.float32)
            grads_out[0, NEAR - 1] = both.astype(jnp.bfloat16)
            near_grads(0).start()

        return carry

    lax.fori_loop(0, 2, earlier_pieces, 0)

    stores = []
    for half in range(2):
        second_pass(half, OWN)
        query_pass(half)
    stores.append(pltpu.make_async_copy(dq_out, dq_hbm, store_sem.at[0]))
    stores[0].start()

    def total_grads(turn, carry):
        half = jnp.where(turn == 0, 1 - first, first)
        for slot in (NEAR, FAR):

            @pl.when(jnp.where(half == 0, s != (n - 2 if slot == FAR else n), s >= slot))
            def _():
                await_grads(half, slot)

        total = (
            grads_own[half]
            + grads_in[half, NEAR].astype(jnp.float32)
            + grads_in[half, FAR].astype(jnp.float32)
        ).astype(jnp.bfloat16)
        dk_out[half] = total[:, :HEAD_SIZE]
        dv_out[half] = total[:, HEAD_SIZE:]
        for copy in grad_stores(half):
            copy.start()
        return carry

    def grad_stores(half):
        piece = pl.ds(half * PIECE, PIECE)
        return [
            pltpu.make_async_copy(dk_out.at[half], dk_hbm.at[piece], store_sem.at[1 + half]),
            pltpu.make_async_copy(dv_out.at[half], dv_hbm.at[piece], store_sem.at[3 + half]),
        ]

    lax.fori_loop(0, 2, total_grads, 0)

    for wanted, copies in forward:

        @pl.when(wanted)
        def _():
            for copy in copies():
                copy.wait_send()

    for which, copy in enumerate(relay()):

        @pl.when(relays & ~at_fold if which == 1 else relays)
        def _():
            copy.wait_send()

    @pl.when(s == n - 4)
    def _():
        onward().wait_send()

    for half in range(2):

        @pl.when(near_wanted(half))
        def _():
            near_grads(half).wait_send()

        @pl.when(far_wanted(half))
        def _():
            far_grads(half).wait_send()

        for copy in grad_stores(half):
            copy.wait()

    for copy in stores:
        copy.wait()


def store_kernel(dq_ref, dk_ref, dv_ref, dq_out, dk_out, dv_out):
    dq_out[...] = dq_ref[...]
    dk_out[...] = dk_ref[...]
    dv_out[...] = dv_ref[...]


def on_device(queries, keys, values, grad_out, starts):
    n = lax.axis_size("seq")
    bf16, f32 = jnp.bfloat16, jnp.float32
    vmem, dma = pltpu.VMEM, pltpu.SemaphoreType.DMA
    anywhere = pl.BlockSpec(memory_space=pl.ANY)
    shapes = (
        jax.ShapeDtypeStruct(queries.shape, bf16),
        jax.ShapeDtypeStruct(keys.shape, bf16),
        jax.ShapeDtypeStruct(values.shape, bf16),
    )
    made = pl.pallas_call(
        functools.partial(kernel, n),
        out_shape=shapes,
        in_specs=[anywhere] * 4 + [pl.BlockSpec(memory_space=pltpu.SMEM)],
        out_specs=(anywhere,) * 3,
        scratch_shapes=[
            vmem((2 * PIECE, 2 * HEAD_SIZE), bf16),
            vmem((2 * PIECE, 2 * HEAD_SIZE), bf16),
            vmem((2, 3, PIECE, HEAD_SIZE), bf16),
            vmem((2, 3, PIECE, HEAD_SIZE), bf16),
            vmem((2, 3, HEAD_SIZE, PIECE), bf16),
            vmem((2, 8, BLOCK), f32),
            vmem((2, 3, 8, BLOCK), f32),
            vmem((PIECE, HEAD_SIZE), bf16),
            vmem((2, LANES, HEAD_SIZE), bf16),
            vmem((2, LANES, HEAD_SIZE), bf16),
            vmem((2, 3, PIECE, LANES), f32),
            vmem((2, 3, PIECE, LANES), f32),
            vmem((2, 3, PIECE, LANES), bf16),
            vmem((2, 3, 8, LANES), f32),
            vmem((2, 2, PIECE, 2 * HEAD_SIZE), bf16),
            vmem((2, 3, PIECE, 2 * HEAD_SIZE), bf16),
            vmem((2, PIECE, 2 * HEAD_SIZE), f32),
            vmem((2 * PIECE, 2 * HEAD_SIZE), bf16),
            vmem((2, PIECE, HEAD_SIZE), bf16),
            vmem((2, PIECE, HEAD_SIZE), bf16),
            dma((6,)),
            dma((5,)),
        ]
        + [dma((3, 2))] * 6 + [dma((2, 2))] * 2,
        compiler_params=pltpu.CompilerParams(
            collective_id=0, has_side_effects=True, vmem_limit_bytes=58 << 20
        ),
    )(queries, grad_out, keys, values, starts)
    whole = pl.BlockSpec(memory_space=pltpu.VMEM)
    return pl.pallas_call(store_kernel, out_shape=shapes, in_specs=[whole] * 3, out_specs=(whole,) * 3)(*made)


def solution(mesh):
    in_specs = (P("seq", "head"), P("seq", "head"), P("seq", "head"), P("seq", "head"), P("seq"))
    out_specs = (P("seq", "head"), P("seq", "head"), P("seq", "head"))
    return jax.shard_map(
        on_device, mesh=mesh, in_specs=in_specs, out_specs=out_specs, check_vma=False
    )
```

```python
import functools

import jax
import jax.numpy as jnp
from jax import lax
from jax.experimental import pallas as pl
from jax.experimental.pallas import tpu as pltpu
from jax.sharding import PartitionSpec as P

HEAD_SIZE = 128
BLOCK = 128
PIECE = 512
BLOCKS = PIECE // BLOCK
HEADS = 2
TILE = HEADS * BLOCK
LANES = BLOCKS * TILE
OWN, NEAR, FAR = 0, 1, 2
MASKED = -1e30
MESH = pl.DeviceIdType.MESH

query_scaling = 168.0 ** (-0.5)
exp2_scaling = query_scaling * 1.4426950408889634


def span(chunk, i):
    if chunk == OWN:
        return range(i + 1)
    if chunk == FAR:
        return range(i, BLOCKS)
    return range(BLOCKS)


def rows_of(j):
    return slice(j * BLOCK, (j + 1) * BLOCK)


def lanes_of(i):
    return slice(i * TILE, (i + 1) * TILE)


def last_dims(a, b):
    return lax.dot_general(a, b, (((1,), (1,)), ((), ())), preferred_element_type=jnp.float32)


def kernel(
    n, q_hbm, g_hbm, k_hbm, v_hbm, starts, dq_out, dk_out, dv_out,
    q_in, g_in, k_all, v_all, k_t, table, tables, k_hop, q_cat, g_cat, terms, dweights, dscores, stats,
    grads_out, grads_in, grads_own,
    load_sem, k_send, v_send, t_send, k_recv, v_recv, t_recv, g_send, g_recv,
):
    s = lax.axis_index("seq")
    head = lax.axis_index("head")

    loads = [
        pltpu.make_async_copy(q_hbm, q_in, load_sem.at[0]),
        pltpu.make_async_copy(g_hbm, g_in, load_sem.at[1]),
    ]
    for half in range(2):
        piece = pl.ds(half * PIECE, PIECE)
        loads.append(pltpu.make_async_copy(k_hbm.at[piece], k_all.at[half, OWN], load_sem.at[2 + 2 * half]))
        loads.append(pltpu.make_async_copy(v_hbm.at[piece], v_all.at[half, OWN], load_sem.at[3 + 2 * half]))
    for copy in loads:
        copy.start()

    barrier = pltpu.get_barrier_semaphore()
    for step in (-2, -1, 1, 2):
        there = s + step

        @pl.when((there >= 0) & (there < n))
        def _():
            pl.semaphore_signal(barrier, inc=1, device_id=(there, head), device_id_type=MESH)

    for half in range(2):
        own = [starts[half * BLOCKS + j].astype(jnp.float32) for j in range(BLOCKS)]
        line = lax.broadcasted_iota(jnp.int32, (8, BLOCK), 0)
        after = jnp.zeros((8, BLOCK), jnp.float32)
        for j in range(BLOCKS):
            after = after + jnp.where((line < j) | (line == BLOCKS), own[j], 0.0)
        table[half] = after

    @pl.when(s == n - 2)
    def _():
        grads_in[0, FAR] = jnp.zeros((PIECE, 2 * HEAD_SIZE), jnp.bfloat16)

    @pl.when(s == 0)
    def _():
        k_all[0, NEAR] = jnp.zeros((PIECE, HEAD_SIZE), jnp.bfloat16)
        v_all[0, NEAR] = jnp.zeros((PIECE, HEAD_SIZE), jnp.bfloat16)
        tables[0, NEAR] = jnp.ones((8, BLOCK), jnp.float32)
        grads_in[1, NEAR] = jnp.zeros((PIECE, 2 * HEAD_SIZE), jnp.bfloat16)

    @pl.when(s <= 1)
    def _():
        k_all[0, FAR] = jnp.zeros((PIECE, HEAD_SIZE), jnp.bfloat16)
        v_all[0, FAR] = jnp.zeros((PIECE, HEAD_SIZE), jnp.bfloat16)
        tables[0, FAR] = jnp.ones((8, BLOCK), jnp.float32)
        grads_in[1, FAR] = jnp.zeros((PIECE, 2 * HEAD_SIZE), jnp.bfloat16)

    pl.semaphore_wait(barrier, jnp.minimum(s, 2) + jnp.minimum(n - 1 - s, 2))

    folded = s > n - 3
    beyond = jnp.where(folded, 2 * n - 3 - s, s + 2)
    at_fold = s == n - 1
    odd = s % 2 == 1
    first = jnp.where(odd, 0, 1)

    def send_piece(sources, sinks, sends, recvs, there):
        return [
            pltpu.make_async_remote_copy(*refs, device_id=(there, head), device_id_type=MESH)
            for refs in zip(sources, sinks, sends, recvs)
        ]

    def at(refs, *index):
        return [ref.at[index] for ref in refs]

    pieces, sends, recvs = (tables, k_all, v_all), (t_send, k_send, v_send), (t_recv, k_recv, v_recv)

    def own_refs(half):
        piece = pl.ds(half * PIECE, PIECE)
        return table.at[half], k_hbm.at[piece], v_hbm.at[piece]

    def own_piece(half, slot, there):
        return send_piece(
            own_refs(half), at(pieces, half, slot), at(sends, half, slot - 1), at(recvs, half, slot - 1), there)

    def held_piece(half, there):
        return send_piece(
            at(pieces, half, FAR), at(pieces, half, NEAR), at(sends, 2, 0), at(recvs, half, NEAR - 1), there)

    def sidestep():
        return pltpu.make_async_remote_copy(
            own_refs(0)[1], k_hop, k_send.at[2, 1], k_recv.at[2, 0],
            device_id=(n - 4, head), device_id_type=MESH)

    def onward():
        return pltpu.make_async_remote_copy(
            k_hop, k_all.at[0, NEAR], k_send.at[2, 1], k_recv.at[0, NEAR - 1],
            device_id=(n - 2, head), device_id_type=MESH)

    def folded_piece():
        return send_piece(
            own_refs(0), at(pieces, 1, FAR), at(sends, 0, FAR - 1), at(recvs, 1, FAR - 1), n - 2)

    def pass_grads(half, slot, there, to_half):
        return pltpu.make_async_remote_copy(
            grads_out.at[half, slot - 1], grads_in.at[to_half, slot], g_send.at[half, slot - 1],
            g_recv.at[to_half, slot - 1], device_id=(there, head), device_id_type=MESH)

    forward = [
        (~odd, lambda: own_piece(0, NEAR, s + 1)),
        (odd, lambda: own_piece(1, NEAR, s - 1)),
        (at_fold, folded_piece),
        (s == n - 3, lambda: [sidestep()]),
        (s <= n - 3, lambda: own_piece(0, FAR, s + 2)),
        (s >= 2, lambda: own_piece(1, FAR, s - 2)),
    ]
    relays = jnp.where(odd, s >= 3, s <= n - 4)
    relay = lambda: held_piece(jnp.where(odd, 0, 1), jnp.where(odd, s - 1, s + 1))
    across = [
        pltpu.make_async_copy(table.at[0], tables.at[1, NEAR], t_recv.at[1, 0]),
        pltpu.make_async_copy(k_hbm.at[pl.ds(0, PIECE)], k_all.at[1, NEAR], k_recv.at[1, 0]),
        pltpu.make_async_copy(v_hbm.at[pl.ds(0, PIECE)], v_all.at[1, NEAR], v_recv.at[1, 0]),
    ]
    again = [
        pltpu.make_async_copy(kept.at[0, NEAR], kept.at[1, FAR], sem.at[1, 1])
        for kept, sem in ((tables, t_recv), (k_all, k_recv), (v_all, v_recv))
    ]
    for wanted, copies in forward:

        @pl.when(wanted)
        def _():
            for copy in copies():
                copy.start()

    @pl.when(at_fold)
    def _():
        for copy in across:
            copy.start()

    for copy in loads:
        copy.wait()

    for half in range(2):
        for i in range(BLOCKS):
            for h in range(HEADS):
                rows = slice(half * PIECE + i * BLOCK, half * PIECE + (i + 1) * BLOCK)
                to = slice(i * TILE + h * BLOCK, i * TILE + (h + 1) * BLOCK)
                cols = slice(h * HEAD_SIZE, (h + 1) * HEAD_SIZE)
                q_cat[half, to, :] = q_in[rows, cols]
                g_cat[half, to, :] = g_in[rows, cols]

    key_row = lax.broadcasted_iota(jnp.int32, (BLOCK, TILE), 0)
    query_row = lax.broadcasted_iota(jnp.int32, (BLOCK, TILE), 1) % BLOCK
    causal = key_row <= query_row

    def first_pass(half, chunk):
        k_t[half, chunk] = k_all[half, chunk].T
        for i in range(BLOCKS):
            begun = [starts[half * BLOCKS + j] for j in range(BLOCKS)]
            q_i = q_cat[half, lanes_of(i), :]
            g_i = g_cat[half, lanes_of(i), :]
            scores = []
            for j in span(chunk, i):
                x = last_dims(k_all[half, chunk, rows_of(j), :], q_i) * exp2_scaling
                if chunk == OWN:
                    count = functools.reduce(lambda a, b: a + b, begun[j + 1 : i + 1], jnp.int32(0))
                    since = jnp.full((1, BLOCK), count.astype(jnp.float32))
                else:
                    count = functools.reduce(lambda a, b: a + b, begun[: i + 1])
                    since = tables[half, chunk, j : j + 1, :] + count.astype(jnp.float32)
                    if chunk == FAR:
                        since = since + tables[half, NEAR, BLOCKS : BLOCKS + 1, :]
                if not (chunk == OWN and j == i):
                    bias = jnp.where(since > 0.5, MASKED, 0.0)
                    x = x + jnp.concatenate([bias, bias], axis=1)
                if chunk == OWN and j == i:
                    x = jnp.where(causal, x, MASKED)
                if chunk == FAR and j == i:
                    x = jnp.where(causal, MASKED, x)
                scores.append(x)
            top = functools.reduce(jnp.maximum, [jnp.max(x, axis=0, keepdims=True) for x in scores])
            total = jnp.zeros((1, TILE), jnp.float32)
            dotted = jnp.zeros((1, TILE), jnp.float32)
            for j, x in zip(span(chunk, i), scores):
                e = jnp.exp2(x - top)
                w = last_dims(v_all[half, chunk, rows_of(j), :], g_i)
                total = total + jnp.sum(e, axis=0, keepdims=True)
                dotted = dotted + jnp.sum(e * w, axis=0, keepdims=True)
                terms[half, chunk, rows_of(j), lanes_of(i)] = e
                dweights[half, chunk, rows_of(j), lanes_of(i)] = w
            stats[half, chunk, 0:1, lanes_of(i)] = top
            stats[half, chunk, 1:2, lanes_of(i)] = total
            stats[half, chunk, 2:3, lanes_of(i)] = dotted

    def merge(half):
        tops = [stats[half, c, 0:1, :] for c in range(3)]
        top = functools.reduce(jnp.maximum, tops)
        ratios = [jnp.exp2(t - top) for t in tops]
        total = sum(stats[half, c, 1:2, :] * ratios[c] for c in range(3))
        dotted = sum(stats[half, c, 2:3, :] * ratios[c] for c in range(3))
        inverse = 1.0 / total
        for c in range(3):
            stats[half, c, 3:4, :] = ratios[c] * inverse
        stats[half, OWN, 4:5, :] = dotted * inverse

    def second_pass(half, chunk):
        for j in range(BLOCKS):
            dk = jnp.zeros((BLOCK, HEAD_SIZE), jnp.float32)
            dv = jnp.zeros((BLOCK, HEAD_SIZE), jnp.float32)
            for i in range(BLOCKS):
                if j not in span(chunk, i):
                    continue
                p = terms[half, chunk, rows_of(j), lanes_of(i)] * stats[half, chunk, 3:4, lanes_of(i)]
                d = p * (dweights[half, chunk, rows_of(j), lanes_of(i)] - stats[half, OWN, 4:5, lanes_of(i)])
                d = d.astype(jnp.bfloat16)
                dscores[half, chunk, rows_of(j), lanes_of(i)] = d
                dk = dk + jnp.dot(d, q_cat[half, lanes_of(i), :], preferred_element_type=jnp.float32)
                dv = dv + jnp.dot(
                    p.astype(jnp.bfloat16), g_cat[half, lanes_of(i), :], preferred_element_type=jnp.float32)
            both = jnp.concatenate([dk * query_scaling, dv], axis=1)
            if chunk == OWN:
                grads_own[half, rows_of(j), :] = both
            else:
                grads_out[half, chunk - 1, rows_of(j), :] = both.astype(jnp.bfloat16)

    def query_pass(half):
        for i in range(BLOCKS):
            total = jnp.zeros((HEAD_SIZE, TILE), jnp.float32)
            for c in range(3):
                js = span(c, i)
                keys = slice(js[0] * BLOCK, (js[-1] + 1) * BLOCK)
                total = total + jnp.dot(
                    k_t[half, c, :, keys], dscores[half, c, keys, lanes_of(i)], preferred_element_type=jnp.float32)
            turned = (total * query_scaling).T.astype(jnp.bfloat16)
            rows = pl.ds(half * PIECE + i * BLOCK, BLOCK)
            for h in range(HEADS):
                dq_out[rows, h * HEAD_SIZE : (h + 1) * HEAD_SIZE] = turned[h * BLOCK : (h + 1) * BLOCK, :]

    def await_piece(half, slot):
        return [
            pltpu.make_async_copy(*refs)
            for refs in zip(own_refs(0), at(pieces, half, slot), at(recvs, half, slot - 1))
        ]

    def await_grads(half, slot):
        pltpu.make_async_copy(grads_out.at[0, 0], grads_in.at[half, slot], g_recv.at[half, slot - 1]).wait()

    def near_grads(half):
        return pass_grads(half, NEAR, jnp.where(half == 0, s - 1, s + 1), half)

    def far_grads(half):
        there = jnp.where(half == 0, s - 2, beyond)
        return pass_grads(half, FAR, there, jnp.where((half == 0) | folded, 0, 1))

    def near_wanted(half):
        return jnp.where(half == 0, s >= 1, s < n - 1)

    def far_wanted(half):
        return jnp.where(half == 0, s >= 2, s < n - 1)

    home = pltpu.make_async_copy(grads_out.at[1, 0], grads_in.at[0, NEAR], g_recv.at[0, 0])

    for half in range(2):
        first_pass(half, OWN)

    def earlier_pieces(turn, carry):
        half = jnp.where(turn == 0, first, 1 - first)

        @pl.when((half == 1) | (s >= 2))
        def _():
            for which, (awaited, copy) in enumerate(zip(await_piece(half, FAR), relay())):
                awaited.wait()
                able = relays & ~at_fold if which == 1 else relays

                @pl.when(able & (turn == 0))
                def _():
                    copy.start()

        @pl.when((s == n - 4) & (turn == 0))
        def _():
            pltpu.make_async_copy(own_refs(0)[1], k_hop, k_recv.at[2, 0]).wait()
            onward().start()

        @pl.when((half == 1) | (s >= 1))
        def _():
            await_piece(half, NEAR)[0].wait()

        first_pass(half, FAR)

        @pl.when((half == 1) | (s >= 1))
        def _():
            for copy in await_piece(half, NEAR)[1:]:
                copy.wait()

        @pl.when(at_fold & (turn == 0))
        def _():
            for copy in again:
                copy.start()

        first_pass(half, NEAR)
        merge(half)
        second_pass(half, NEAR)

        @pl.when(near_wanted(half) & ~(at_fold & (half == 0)))
        def _():
            near_grads(half).start()

        @pl.when(at_fold & (half == 1))
        def _():
            home.start()

        second_pass(half, FAR)

        @pl.when(far_wanted(half))
        def _():
            far_grads(half).start()

        @pl.when(at_fold & (half == 1))
        def _():
            both = grads_out[0, NEAR - 1].astype(jnp.float32) + grads_out[1, FAR - 1].astype(jnp.float32)
            grads_out[0, NEAR - 1] = both.astype(jnp.bfloat16)
            near_grads(0).start()

        return carry

    lax.fori_loop(0, 2, earlier_pieces, 0)

    for half in range(2):
        second_pass(half, OWN)
        query_pass(half)

    def total_grads(turn, carry):
        half = jnp.where(turn == 0, 1 - first, first)
        for slot in (NEAR, FAR):

            @pl.when(jnp.where(half == 0, s != (n - 2 if slot == FAR else n), s >= slot))
            def _():
                await_grads(half, slot)

        total = (
            grads_own[half]
            + grads_in[half, NEAR].astype(jnp.float32)
            + grads_in[half, FAR].astype(jnp.float32)
        ).astype(jnp.bfloat16)
        piece = pl.ds(pl.multiple_of(half * PIECE, PIECE), PIECE)
        dk_out[piece, :] = total[:, :HEAD_SIZE]
        dv_out[piece, :] = total[:, HEAD_SIZE:]
        return carry

    lax.fori_loop(0, 2, total_grads, 0)

    for wanted, copies in forward:

        @pl.when(wanted)
        def _():
            for copy in copies():
                copy.wait_send()

    for which, copy in enumerate(relay()):

        @pl.when(relays & ~at_fold if which == 1 else relays)
        def _():
            copy.wait_send()

    @pl.when(s == n - 4)
    def _():
        onward().wait_send()

    for half in range(2):

        @pl.when(near_wanted(half))
        def _():
            near_grads(half).wait_send()

        @pl.when(far_wanted(half))
        def _():
            far_grads(half).wait_send()


def store_kernel(dq_ref, dk_ref, dv_ref, dq_hbm, dk_hbm, dv_hbm, sems):
    copies = []
    for which, (made, to) in enumerate(((dq_ref, dq_hbm), (dk_ref, dk_hbm), (dv_ref, dv_hbm))):
        for half in range(2):
            piece = pl.ds(half * PIECE, PIECE)
            copies.append(pltpu.make_async_copy(made.at[piece], to.at[piece], sems.at[2 * which + half]))
    for copy in copies:
        copy.start()
    for copy in copies:
        copy.wait()


def on_device(queries, keys, values, grad_out, starts):
    n = lax.axis_size("seq")
    bf16, f32 = jnp.bfloat16, jnp.float32
    vmem, dma = pltpu.VMEM, pltpu.SemaphoreType.DMA
    anywhere = pl.BlockSpec(memory_space=pl.ANY)
    shapes = (
        jax.ShapeDtypeStruct(queries.shape, bf16),
        jax.ShapeDtypeStruct(keys.shape, bf16),
        jax.ShapeDtypeStruct(values.shape, bf16),
    )
    made = pl.pallas_call(
        functools.partial(kernel, n),
        out_shape=shapes,
        in_specs=[anywhere] * 4 + [pl.BlockSpec(memory_space=pltpu.SMEM)],
        out_specs=(pl.BlockSpec(memory_space=pltpu.VMEM),) * 3,
        scratch_shapes=[
            vmem((2 * PIECE, 2 * HEAD_SIZE), bf16),
            vmem((2 * PIECE, 2 * HEAD_SIZE), bf16),
            vmem((2, 3, PIECE, HEAD_SIZE), bf16),
            vmem((2, 3, PIECE, HEAD_SIZE), bf16),
            vmem((2, 3, HEAD_SIZE, PIECE), bf16),
            vmem((2, 8, BLOCK), f32),
            vmem((2, 3, 8, BLOCK), f32),
            vmem((PIECE, HEAD_SIZE), bf16),
            vmem((2, LANES, HEAD_SIZE), bf16),
            vmem((2, LANES, HEAD_SIZE), bf16),
            vmem((2, 3, PIECE, LANES), f32),
            vmem((2, 3, PIECE, LANES), f32),
            vmem((2, 3, PIECE, LANES), bf16),
            vmem((2, 3, 8, LANES), f32),
            vmem((2, 2, PIECE, 2 * HEAD_SIZE), bf16),
            vmem((2, 3, PIECE, 2 * HEAD_SIZE), bf16),
            vmem((2, PIECE, 2 * HEAD_SIZE), f32),
            dma((6,)),
        ]
        + [dma((3, 2))] * 6 + [dma((2, 2))] * 2,
        compiler_params=pltpu.CompilerParams(
            collective_id=0, has_side_effects=True, vmem_limit_bytes=48 << 20
        ),
    )(*(pltpu.with_memory_space_constraint(x, pltpu.HBM) for x in (queries, grad_out, keys, values, starts)))
    return pl.pallas_call(
        store_kernel,
        out_shape=shapes,
        in_specs=[anywhere] * 3,
        out_specs=(pl.BlockSpec(memory_space=pltpu.HBM),) * 3,
        scratch_shapes=[dma((6,))],
        compiler_params=pltpu.CompilerParams(vmem_limit_bytes=1 << 20),
    )(*made)


def solution(mesh):
    in_specs = (P("seq", "head"), P("seq", "head"), P("seq", "head"), P("seq", "head"), P("seq"))
    out_specs = (P("seq", "head"), P("seq", "head"), P("seq", "head"))
    return jax.shard_map(
        on_device, mesh=mesh, in_specs=in_specs, out_specs=out_specs, check_vma=False
    )
```

```python
import functools

import jax
import jax.numpy as jnp
from jax import lax
from jax.experimental import pallas as pl
from jax.experimental.pallas import tpu as pltpu
from jax.sharding import PartitionSpec as P

HEAD_SIZE = 128
BLOCK = 128
PIECE = 512
BLOCKS = PIECE // BLOCK
HEADS = 2
TILE = HEADS * BLOCK
LANES = BLOCKS * TILE
OWN, NEAR, FAR = 0, 1, 2
MASKED = -1e30
MESH = pl.DeviceIdType.MESH

query_scaling = 168.0 ** (-0.5)
exp2_scaling = query_scaling * 1.4426950408889634


def span(chunk, i):
    if chunk == OWN:
        return range(i + 1)
    if chunk == FAR:
        return range(i, BLOCKS)
    return range(BLOCKS)


def rows_of(j):
    return slice(j * BLOCK, (j + 1) * BLOCK)


def lanes_of(i):
    return slice(i * TILE, (i + 1) * TILE)


def last_dims(a, b):
    return lax.dot_general(a, b, (((1,), (1,)), ((), ())), preferred_element_type=jnp.float32)


def kernel(
    n, q_hbm, g_hbm, k_hbm, v_hbm, starts, dq_out, dk_out, dv_out,
    q_in, g_in, k_all, v_all, k_t, table, tables, k_hop, q_cat, g_cat, terms, dweights, dscores, stats,
    grads_out, grads_in, grads_own, g_hop,
    load_sem, k_send, v_send, t_send, k_recv, v_recv, t_recv, g_send, g_recv,
):
    s = lax.axis_index("seq")
    head = lax.axis_index("head")

    loads = [
        pltpu.make_async_copy(q_hbm, q_in, load_sem.at[0]),
        pltpu.make_async_copy(g_hbm, g_in, load_sem.at[1]),
    ]
    for half in range(2):
        piece = pl.ds(half * PIECE, PIECE)
        loads.append(pltpu.make_async_copy(k_hbm.at[piece], k_all.at[half, OWN], load_sem.at[2 + 2 * half]))
        loads.append(pltpu.make_async_copy(v_hbm.at[piece], v_all.at[half, OWN], load_sem.at[3 + 2 * half]))
    for copy in loads:
        copy.start()

    barrier = pltpu.get_barrier_semaphore()
    for step in (-2, -1, 1, 2):
        there = s + step

        @pl.when((there >= 0) & (there < n))
        def _():
            pl.semaphore_signal(barrier, inc=1, device_id=(there, head), device_id_type=MESH)

    for half in range(2):
        own = [starts[half * BLOCKS + j].astype(jnp.float32) for j in range(BLOCKS)]
        line = lax.broadcasted_iota(jnp.int32, (8, BLOCK), 0)
        after = jnp.zeros((8, BLOCK), jnp.float32)
        for j in range(BLOCKS):
            after = after + jnp.where((line < j) | (line == BLOCKS), own[j], 0.0)
        table[half] = after

    @pl.when(s == n - 2)
    def _():
        grads_in[0, FAR] = jnp.zeros((PIECE, 2 * HEAD_SIZE), jnp.bfloat16)

    @pl.when(s == 0)
    def _():
        k_all[0, NEAR] = jnp.zeros((PIECE, HEAD_SIZE), jnp.bfloat16)
        v_all[0, NEAR] = jnp.zeros((PIECE, HEAD_SIZE), jnp.bfloat16)
        tables[0, NEAR] = jnp.ones((8, BLOCK), jnp.float32)
        grads_in[1, NEAR] = jnp.zeros((PIECE, 2 * HEAD_SIZE), jnp.bfloat16)

    @pl.when(s <= 1)
    def _():
        k_all[0, FAR] = jnp.zeros((PIECE, HEAD_SIZE), jnp.bfloat16)
        v_all[0, FAR] = jnp.zeros((PIECE, HEAD_SIZE), jnp.bfloat16)
        tables[0, FAR] = jnp.ones((8, BLOCK), jnp.float32)
        grads_in[1, FAR] = jnp.zeros((PIECE, 2 * HEAD_SIZE), jnp.bfloat16)

    pl.semaphore_wait(barrier, jnp.minimum(s, 2) + jnp.minimum(n - 1 - s, 2))

    folded = s > n - 3
    beyond = jnp.where(folded, 2 * n - 3 - s, s + 2)
    at_fold = s == n - 1
    odd = s % 2 == 1
    first = jnp.where(odd, 0, 1)

    def send_piece(sources, sinks, sends, recvs, there):
        return [
            pltpu.make_async_remote_copy(*refs, device_id=(there, head), device_id_type=MESH)
            for refs in zip(sources, sinks, sends, recvs)
        ]

    def at(refs, *index):
        return [ref.at[index] for ref in refs]

    pieces, sends, recvs = (tables, k_all, v_all), (t_send, k_send, v_send), (t_recv, k_recv, v_recv)

    def own_refs(half):
        piece = pl.ds(half * PIECE, PIECE)
        return table.at[half], k_hbm.at[piece], v_hbm.at[piece]

    def own_piece(half, slot, there):
        return send_piece(
            own_refs(half), at(pieces, half, slot), at(sends, half, slot - 1), at(recvs, half, slot - 1), there)

    def held_piece(half, there):
        return send_piece(
            at(pieces, half, FAR), at(pieces, half, NEAR), at(sends, 2, 0), at(recvs, half, NEAR - 1), there)

    def sidestep():
        return pltpu.make_async_remote_copy(
            own_refs(0)[1], k_hop, k_send.at[2, 1], k_recv.at[2, 0],
            device_id=(n - 4, head), device_id_type=MESH)

    def onward():
        return pltpu.make_async_remote_copy(
            k_hop, k_all.at[0, NEAR], k_send.at[2, 1], k_recv.at[0, NEAR - 1],
            device_id=(n - 2, head), device_id_type=MESH)

    def folded_piece():
        return send_piece(
            own_refs(0), at(pieces, 1, FAR), at(sends, 0, FAR - 1), at(recvs, 1, FAR - 1), n - 2)

    def pass_grads(half, slot, there, to_half):
        return pltpu.make_async_remote_copy(
            grads_out.at[half, slot - 1], grads_in.at[to_half, slot], g_send.at[half, slot - 1],
            g_recv.at[to_half, slot - 1], device_id=(there, head), device_id_type=MESH)

    forward = [
        (~odd, lambda: own_piece(0, NEAR, s + 1)),
        (odd, lambda: own_piece(1, NEAR, s - 1)),
        (at_fold, folded_piece),
        (s == n - 3, lambda: [sidestep()]),
        (s <= n - 3, lambda: own_piece(0, FAR, s + 2)),
        (s >= 2, lambda: own_piece(1, FAR, s - 2)),
    ]
    relays = jnp.where(odd, s >= 3, s <= n - 4)
    relay = lambda: held_piece(jnp.where(odd, 0, 1), jnp.where(odd, s - 1, s + 1))
    across = [
        pltpu.make_async_copy(table.at[0], tables.at[1, NEAR], t_recv.at[1, 0]),
        pltpu.make_async_copy(k_hbm.at[pl.ds(0, PIECE)], k_all.at[1, NEAR], k_recv.at[1, 0]),
        pltpu.make_async_copy(v_hbm.at[pl.ds(0, PIECE)], v_all.at[1, NEAR], v_recv.at[1, 0]),
    ]
    again = [
        pltpu.make_async_copy(kept.at[0, NEAR], kept.at[1, FAR], sem.at[1, 1])
        for kept, sem in ((tables, t_recv), (k_all, k_recv), (v_all, v_recv))
    ]
    for wanted, copies in forward:

        @pl.when(wanted)
        def _():
            for copy in copies():
                copy.start()

    @pl.when(at_fold)
    def _():
        for copy in across:
            copy.start()

    for copy in loads:
        copy.wait()

    for half in range(2):
        for i in range(BLOCKS):
            for h in range(HEADS):
                rows = slice(half * PIECE + i * BLOCK, half * PIECE + (i + 1) * BLOCK)
                to = slice(i * TILE + h * BLOCK, i * TILE + (h + 1) * BLOCK)
                cols = slice(h * HEAD_SIZE, (h + 1) * HEAD_SIZE)
                q_cat[half, to, :] = q_in[rows, cols]
                g_cat[half, to, :] = g_in[rows, cols]

    key_row = lax.broadcasted_iota(jnp.int32, (BLOCK, TILE), 0)
    query_row = lax.broadcasted_iota(jnp.int32, (BLOCK, TILE), 1) % BLOCK
    causal = key_row <= query_row

    def key_pass(half, chunk):
        k_t[half, chunk] = k_all[half, chunk].T
        for i in range(BLOCKS):
            begun = [starts[half * BLOCKS + j] for j in range(BLOCKS)]
            q_i = q_cat[half, lanes_of(i), :]
            scores = []
            for j in span(chunk, i):
                x = last_dims(k_all[half, chunk, rows_of(j), :], q_i) * exp2_scaling
                if chunk == OWN:
                    count = functools.reduce(lambda a, b: a + b, begun[j + 1 : i + 1], jnp.int32(0))
                    since = jnp.full((1, BLOCK), count.astype(jnp.float32))
                else:
                    count = functools.reduce(lambda a, b: a + b, begun[: i + 1])
                    since = tables[half, chunk, j : j + 1, :] + count.astype(jnp.float32)
                    if chunk == FAR:
                        since = since + tables[half, NEAR, BLOCKS : BLOCKS + 1, :]
                if not (chunk == OWN and j == i):
                    bias = jnp.where(since > 0.5, MASKED, 0.0)
                    x = x + jnp.concatenate([bias, bias], axis=1)
                if chunk == OWN and j == i:
                    x = jnp.where(causal, x, MASKED)
                if chunk == FAR and j == i:
                    x = jnp.where(causal, MASKED, x)
                scores.append(x)
            top = functools.reduce(jnp.maximum, [jnp.max(x, axis=0, keepdims=True) for x in scores])
            total = jnp.zeros((1, TILE), jnp.float32)
            for j, x in zip(span(chunk, i), scores):
                e = jnp.exp2(x - top)
                total = total + jnp.sum(e, axis=0, keepdims=True)
                terms[half, chunk, rows_of(j), lanes_of(i)] = e
            stats[half, chunk, 0:1, lanes_of(i)] = top
            stats[half, chunk, 1:2, lanes_of(i)] = total

    def value_pass(half, chunk):
        for i in range(BLOCKS):
            g_i = g_cat[half, lanes_of(i), :]
            dotted = jnp.zeros((1, TILE), jnp.float32)
            for j in span(chunk, i):
                w = last_dims(v_all[half, chunk, rows_of(j), :], g_i)
                dotted = dotted + jnp.sum(terms[half, chunk, rows_of(j), lanes_of(i)] * w, axis=0, keepdims=True)
                dweights[half, chunk, rows_of(j), lanes_of(i)] = w
            stats[half, chunk, 2:3, lanes_of(i)] = dotted

    def first_pass(half, chunk):
        key_pass(half, chunk)
        value_pass(half, chunk)

    def merge(half):
        tops = [stats[half, c, 0:1, :] for c in range(3)]
        top = functools.reduce(jnp.maximum, tops)
        ratios = [jnp.exp2(t - top) for t in tops]
        total = sum(stats[half, c, 1:2, :] * ratios[c] for c in range(3))
        dotted = sum(stats[half, c, 2:3, :] * ratios[c] for c in range(3))
        inverse = 1.0 / total
        for c in range(3):
            stats[half, c, 3:4, :] = ratios[c] * inverse
        stats[half, OWN, 4:5, :] = dotted * inverse

    def second_pass(half, chunk, blocks=range(BLOCKS)):
        for j in blocks:
            dk = jnp.zeros((BLOCK, HEAD_SIZE), jnp.float32)
            dv = jnp.zeros((BLOCK, HEAD_SIZE), jnp.float32)
            for i in range(BLOCKS):
                if j not in span(chunk, i):
                    continue
                p = terms[half, chunk, rows_of(j), lanes_of(i)] * stats[half, chunk, 3:4, lanes_of(i)]
                d = p * (dweights[half, chunk, rows_of(j), lanes_of(i)] - stats[half, OWN, 4:5, lanes_of(i)])
                d = d.astype(jnp.bfloat16)
                dscores[half, chunk, rows_of(j), lanes_of(i)] = d
                dk = dk + jnp.dot(d, q_cat[half, lanes_of(i), :], preferred_element_type=jnp.float32)
                dv = dv + jnp.dot(
                    p.astype(jnp.bfloat16), g_cat[half, lanes_of(i), :], preferred_element_type=jnp.float32)
            both = jnp.concatenate([dk * query_scaling, dv], axis=1)
            if chunk == OWN:
                grads_own[half, rows_of(j), :] = both
            else:
                grads_out[half, chunk - 1, rows_of(j), :] = both.astype(jnp.bfloat16)

    def query_pass(half):
        for i in range(BLOCKS):
            total = jnp.zeros((HEAD_SIZE, TILE), jnp.float32)
            for c in range(3):
                js = span(c, i)
                keys = slice(js[0] * BLOCK, (js[-1] + 1) * BLOCK)
                total = total + jnp.dot(
                    k_t[half, c, :, keys], dscores[half, c, keys, lanes_of(i)], preferred_element_type=jnp.float32)
            turned = (total * query_scaling).T.astype(jnp.bfloat16)
            rows = pl.ds(half * PIECE + i * BLOCK, BLOCK)
            for h in range(HEADS):
                dq_out[rows, h * HEAD_SIZE : (h + 1) * HEAD_SIZE] = turned[h * BLOCK : (h + 1) * BLOCK, :]

    def await_piece(half, slot):
        return [
            pltpu.make_async_copy(*refs)
            for refs in zip(own_refs(0), at(pieces, half, slot), at(recvs, half, slot - 1))
        ]

    def await_near(half):
        for part in range(2):
            rows = part_rows(part)
            pltpu.make_async_copy(
                grads_out.at[0, 0, rows], grads_in.at[half, NEAR, rows], g_recv.at[2 * part + half, 0]).wait()

    def await_grads(half, slot):
        pltpu.make_async_copy(grads_out.at[0, 0], grads_in.at[half, slot], g_recv.at[half, slot - 1]).wait()

    def part_rows(part):
        return pl.ds(part * (PIECE // 2), PIECE // 2)

    def near_grads(half, part):
        rows = part_rows(part)
        return pltpu.make_async_remote_copy(
            grads_out.at[half, NEAR - 1, rows], grads_in.at[half, NEAR, rows], g_send.at[2 * part + half, 0],
            g_recv.at[2 * part + half, 0], device_id=(jnp.where(half == 0, s - 1, s + 1), head), device_id_type=MESH)

    def far_grads(half):
        there = jnp.where(half == 0, s - 2, beyond)
        return pass_grads(half, FAR, there, jnp.where((half == 0) | folded, 0, 1))

    def near_wanted(half):
        return jnp.where(half == 0, s >= 1, s < n - 1)

    def far_wanted(half):
        return jnp.where(half == 0, s >= 2, s < n - 1)

    def near_aside():
        return pltpu.make_async_remote_copy(
            grads_out.at[0, NEAR - 1, part_rows(1)], g_hop, g_send.at[2, 1], g_recv.at[2, 1],
            device_id=(n - 1, head), device_id_type=MESH)

    def near_onward():
        return pltpu.make_async_remote_copy(
            g_hop, grads_in.at[0, NEAR, part_rows(1)], g_send.at[3, 1], g_recv.at[2, 0],
            device_id=(n - 3, head), device_id_type=MESH)

    before_fold = s == n - 2

    def home(part):
        rows = part_rows(part)
        return pltpu.make_async_copy(
            grads_out.at[1, NEAR - 1, rows], grads_in.at[0, NEAR, rows], g_recv.at[2 * part, 0])

    for half in range(2):
        first_pass(half, OWN)

    def earlier_pieces(turn, carry):
        half = jnp.where(turn == 0, first, 1 - first)

        @pl.when((half == 1) | (s >= 2))
        def _():
            for which, (awaited, copy) in enumerate(zip(await_piece(half, FAR), relay())):
                awaited.wait()
                able = relays & ~at_fold if which == 1 else relays

                @pl.when(able & (turn == 0))
                def _():
                    copy.start()

        @pl.when((s == n - 4) & (turn == 0))
        def _():
            pltpu.make_async_copy(own_refs(0)[1], k_hop, k_recv.at[2, 0]).wait()
            onward().start()

        @pl.when((half == 1) | (s >= 1))
        def _():
            await_piece(half, NEAR)[0].wait()

        first_pass(half, FAR)

        @pl.when((half == 1) | (s >= 1))
        def _():
            await_piece(half, NEAR)[1].wait()

        key_pass(half, NEAR)

        @pl.when((half == 1) | (s >= 1))
        def _():
            await_piece(half, NEAR)[2].wait()

        @pl.when(at_fold & (turn == 0))
        def _():
            for copy in again:
                copy.start()

        value_pass(half, NEAR)
        merge(half)
        def near_block():
            for part in range(2):
                second_pass(half, NEAR, range(part * BLOCKS // 2, (part + 1) * BLOCKS // 2))

                through = before_fold & (half == 0) & (part == 1)

                @pl.when(near_wanted(half) & ~(at_fold & (half == 0)) & ~through)
                def _():
                    near_grads(half, part).start()

                @pl.when(through)
                def _():
                    near_aside().start()
                    far_grads(1).start()

                @pl.when(at_fold & (half == 1))
                def _():
                    home(part).start()

        def far_block():
            second_pass(half, FAR)

            @pl.when(far_wanted(half) & ~(before_fold & (half == 1)))
            def _():
                far_grads(half).start()

        near_block()
        far_block()

        @pl.when(at_fold & (half == 1))
        def _():
            both = grads_out[0, NEAR - 1].astype(jnp.float32) + grads_out[1, FAR - 1].astype(jnp.float32)
            grads_out[0, NEAR - 1] = both.astype(jnp.bfloat16)
            for part in range(2):
                near_grads(0, part).start()

        return carry

    lax.fori_loop(0, 2, earlier_pieces, 0)

    for half in range(2):
        second_pass(half, OWN)
        query_pass(half)

    @pl.when(at_fold)
    def _():
        pltpu.make_async_copy(grads_out.at[0, 0, part_rows(0)], g_hop, g_recv.at[2, 1]).wait()
        near_onward().start()

    def total_grads(turn, carry):
        half = jnp.where(turn == 0, 1 - first, first)
        @pl.when((half == 0) | (s >= 1))
        def _():
            await_near(half)

        @pl.when(jnp.where(half == 0, s != n - 2, s >= 2))
        def _():
            await_grads(half, FAR)

        total = (
            grads_own[half]
            + grads_in[half, NEAR].astype(jnp.float32)
            + grads_in[half, FAR].astype(jnp.float32)
        ).astype(jnp.bfloat16)
        piece = pl.ds(pl.multiple_of(half * PIECE, PIECE), PIECE)
        dk_out[piece, :] = total[:, :HEAD_SIZE]
        dv_out[piece, :] = total[:, HEAD_SIZE:]
        return carry

    lax.fori_loop(0, 2, total_grads, 0)

    for wanted, copies in forward:

        @pl.when(wanted)
        def _():
            for copy in copies():
                copy.wait_send()

    for which, copy in enumerate(relay()):

        @pl.when(relays & ~at_fold if which == 1 else relays)
        def _():
            copy.wait_send()

    @pl.when(s == n - 4)
    def _():
        onward().wait_send()

    @pl.when(at_fold)
    def _():
        near_onward().wait_send()

    for half in range(2):

        @pl.when(near_wanted(half))
        def _():
            near_grads(half, 0).wait_send()

        through = before_fold & (half == 0)

        @pl.when(near_wanted(half) & ~through)
        def _():
            near_grads(half, 1).wait_send()

        @pl.when(through)
        def _():
            near_aside().wait_send()

        @pl.when(far_wanted(half))
        def _():
            far_grads(half).wait_send()


def store_kernel(dq_ref, dk_ref, dv_ref, dq_hbm, dk_hbm, dv_hbm, sems):
    copies = []
    for which, (made, to) in enumerate(((dq_ref, dq_hbm), (dk_ref, dk_hbm), (dv_ref, dv_hbm))):
        for half in range(2):
            piece = pl.ds(half * PIECE, PIECE)
            copies.append(pltpu.make_async_copy(made.at[piece], to.at[piece], sems.at[2 * which + half]))
    for copy in copies:
        copy.start()
    for copy in copies:
        copy.wait()


def on_device(queries, keys, values, grad_out, starts):
    n = lax.axis_size("seq")
    bf16, f32 = jnp.bfloat16, jnp.float32
    vmem, dma = pltpu.VMEM, pltpu.SemaphoreType.DMA
    anywhere = pl.BlockSpec(memory_space=pl.ANY)
    shapes = (
        jax.ShapeDtypeStruct(queries.shape, bf16),
        jax.ShapeDtypeStruct(keys.shape, bf16),
        jax.ShapeDtypeStruct(values.shape, bf16),
    )
    made = pl.pallas_call(
        functools.partial(kernel, n),
        out_shape=shapes,
        in_specs=[anywhere] * 4 + [pl.BlockSpec(memory_space=pltpu.SMEM)],
        out_specs=(pl.BlockSpec(memory_space=pltpu.VMEM),) * 3,
        scratch_shapes=[
            vmem((2 * PIECE, 2 * HEAD_SIZE), bf16),
            vmem((2 * PIECE, 2 * HEAD_SIZE), bf16),
            vmem((2, 3, PIECE, HEAD_SIZE), bf16),
            vmem((2, 3, PIECE, HEAD_SIZE), bf16),
            vmem((2, 3, HEAD_SIZE, PIECE), bf16),
            vmem((2, 8, BLOCK), f32),
            vmem((2, 3, 8, BLOCK), f32),
            vmem((PIECE, HEAD_SIZE), bf16),
            vmem((2, LANES, HEAD_SIZE), bf16),
            vmem((2, LANES, HEAD_SIZE), bf16),
            vmem((2, 3, PIECE, LANES), f32),
            vmem((2, 3, PIECE, LANES), f32),
            vmem((2, 3, PIECE, LANES), bf16),
            vmem((2, 3, 8, LANES), f32),
            vmem((2, 2, PIECE, 2 * HEAD_SIZE), bf16),
            vmem((2, 3, PIECE, 2 * HEAD_SIZE), bf16),
            vmem((2, PIECE, 2 * HEAD_SIZE), f32),
            vmem((PIECE // 2, 2 * HEAD_SIZE), bf16),
            dma((6,)),
        ]
        + [dma((3, 2))] * 6 + [dma((4, 2))] * 2,
        compiler_params=pltpu.CompilerParams(
            collective_id=0, has_side_effects=True, vmem_limit_bytes=48 << 20
        ),
    )(*(pltpu.with_memory_space_constraint(x, pltpu.HBM) for x in (queries, grad_out, keys, values, starts)))
    return pl.pallas_call(
        store_kernel,
        out_shape=shapes,
        in_specs=[anywhere] * 3,
        out_specs=(pl.BlockSpec(memory_space=pltpu.HBM),) * 3,
        scratch_shapes=[dma((6,))],
        compiler_params=pltpu.CompilerParams(vmem_limit_bytes=1 << 20),
    )(*made)


def solution(mesh):
    in_specs = (P("seq", "head"), P("seq", "head"), P("seq", "head"), P("seq", "head"), P("seq"))
    out_specs = (P("seq", "head"), P("seq", "head"), P("seq", "head"))
    return jax.shard_map(
        on_device, mesh=mesh, in_specs=in_specs, out_specs=out_specs, check_vma=False
    )
```

```python
import functools

import jax
import jax.numpy as jnp
from jax import lax
from jax.experimental import pallas as pl
from jax.experimental.pallas import tpu as pltpu
from jax.sharding import PartitionSpec as P

HEAD_SIZE = 128
BLOCK = 128
PIECE = 512
BLOCKS = PIECE // BLOCK
LARGER = 3
HEADS = 2
TILE = HEADS * BLOCK
LANES = BLOCKS * TILE
OWN, NEAR, FAR = 0, 1, 2
MASKED = -1e30
MESH = pl.DeviceIdType.MESH

query_scaling = 168.0 ** (-0.5)
exp2_scaling = query_scaling * 1.4426950408889634


def span(chunk, i):
    if chunk == OWN:
        return range(i + 1)
    if chunk == FAR:
        return range(i, BLOCKS)
    return range(BLOCKS)


def rows_of(j):
    return slice(j * BLOCK, (j + 1) * BLOCK)


def lanes_of(i):
    return slice(i * TILE, (i + 1) * TILE)


def last_dims(a, b):
    return lax.dot_general(a, b, (((1,), (1,)), ((), ())), preferred_element_type=jnp.float32)


def kernel(
    n, q_hbm, g_hbm, k_hbm, v_hbm, starts, dq_out, dk_out, dv_out,
    q_in, g_in, k_all, v_all, k_t, table, tables, k_hop, q_cat, g_cat, terms, dweights, dscores, stats,
    grads_out, grads_in, grads_own, g_hop,
    load_sem, k_send, v_send, t_send, k_recv, v_recv, t_recv, g_send, g_recv,
):
    s = lax.axis_index("seq")
    head = lax.axis_index("head")

    loads = [
        pltpu.make_async_copy(q_hbm, q_in, load_sem.at[0]),
        pltpu.make_async_copy(g_hbm, g_in, load_sem.at[1]),
    ]
    for half in range(2):
        piece = pl.ds(half * PIECE, PIECE)
        loads.append(pltpu.make_async_copy(k_hbm.at[piece], k_all.at[half, OWN], load_sem.at[2 + 2 * half]))
        loads.append(pltpu.make_async_copy(v_hbm.at[piece], v_all.at[half, OWN], load_sem.at[3 + 2 * half]))
    for copy in loads:
        copy.start()

    barrier = pltpu.get_barrier_semaphore()
    for step in (-2, -1, 1, 2):
        there = s + step

        @pl.when((there >= 0) & (there < n))
        def _():
            pl.semaphore_signal(barrier, inc=1, device_id=(there, head), device_id_type=MESH)

    for half in range(2):
        own = [starts[half * BLOCKS + j].astype(jnp.float32) for j in range(BLOCKS)]
        line = lax.broadcasted_iota(jnp.int32, (8, BLOCK), 0)
        after = jnp.zeros((8, BLOCK), jnp.float32)
        for j in range(BLOCKS):
            after = after + jnp.where((line < j) | (line == BLOCKS), own[j], 0.0)
        table[half] = after

    @pl.when(s == n - 2)
    def _():
        grads_in[0, FAR] = jnp.zeros((PIECE, 2 * HEAD_SIZE), jnp.bfloat16)

    @pl.when(s == 0)
    def _():
        k_all[0, NEAR] = jnp.zeros((PIECE, HEAD_SIZE), jnp.bfloat16)
        v_all[0, NEAR] = jnp.zeros((PIECE, HEAD_SIZE), jnp.bfloat16)
        tables[0, NEAR] = jnp.ones((8, BLOCK), jnp.float32)
        grads_in[1, NEAR] = jnp.zeros((PIECE, 2 * HEAD_SIZE), jnp.bfloat16)

    @pl.when(s <= 1)
    def _():
        k_all[0, FAR] = jnp.zeros((PIECE, HEAD_SIZE), jnp.bfloat16)
        v_all[0, FAR] = jnp.zeros((PIECE, HEAD_SIZE), jnp.bfloat16)
        tables[0, FAR] = jnp.ones((8, BLOCK), jnp.float32)
        grads_in[1, FAR] = jnp.zeros((PIECE, 2 * HEAD_SIZE), jnp.bfloat16)

    pl.semaphore_wait(barrier, jnp.minimum(s, 2) + jnp.minimum(n - 1 - s, 2))

    folded = s > n - 3
    beyond = jnp.where(folded, 2 * n - 3 - s, s + 2)
    at_fold = s == n - 1
    odd = s % 2 == 1
    first = jnp.where(odd, 0, 1)

    def send_piece(sources, sinks, sends, recvs, there):
        return [
            pltpu.make_async_remote_copy(*refs, device_id=(there, head), device_id_type=MESH)
            for refs in zip(sources, sinks, sends, recvs)
        ]

    def at(refs, *index):
        return [ref.at[index] for ref in refs]

    pieces, sends, recvs = (tables, k_all, v_all), (t_send, k_send, v_send), (t_recv, k_recv, v_recv)

    def own_refs(half):
        piece = pl.ds(half * PIECE, PIECE)
        return table.at[half], k_hbm.at[piece], v_hbm.at[piece]

    def own_piece(half, slot, there):
        return send_piece(
            own_refs(half), at(pieces, half, slot), at(sends, half, slot - 1), at(recvs, half, slot - 1), there)

    def held_piece(half, there):
        return send_piece(
            at(pieces, half, FAR), at(pieces, half, NEAR), at(sends, 2, 0), at(recvs, half, NEAR - 1), there)

    def sidestep():
        return pltpu.make_async_remote_copy(
            own_refs(0)[1], k_hop, k_send.at[2, 1], k_recv.at[2, 0],
            device_id=(n - 4, head), device_id_type=MESH)

    def onward():
        return pltpu.make_async_remote_copy(
            k_hop, k_all.at[0, NEAR], k_send.at[2, 1], k_recv.at[0, NEAR - 1],
            device_id=(n - 2, head), device_id_type=MESH)

    def folded_piece():
        return send_piece(
            own_refs(0), at(pieces, 1, FAR), at(sends, 0, FAR - 1), at(recvs, 1, FAR - 1), n - 2)

    def pass_grads(half, slot, there, to_half):
        return pltpu.make_async_remote_copy(
            grads_out.at[half, slot - 1], grads_in.at[to_half, slot], g_send.at[half, slot - 1],
            g_recv.at[to_half, slot - 1], device_id=(there, head), device_id_type=MESH)

    forward = [
        (~odd, lambda: own_piece(0, NEAR, s + 1)),
        (odd, lambda: own_piece(1, NEAR, s - 1)),
        (at_fold, folded_piece),
        (s == n - 3, lambda: [sidestep()]),
        (s <= n - 3, lambda: own_piece(0, FAR, s + 2)),
        (s >= 2, lambda: own_piece(1, FAR, s - 2)),
    ]
    relays = jnp.where(odd, s >= 3, s <= n - 4)
    relay = lambda: held_piece(jnp.where(odd, 0, 1), jnp.where(odd, s - 1, s + 1))
    across = [
        pltpu.make_async_copy(table.at[0], tables.at[1, NEAR], t_recv.at[1, 0]),
        pltpu.make_async_copy(k_hbm.at[pl.ds(0, PIECE)], k_all.at[1, NEAR], k_recv.at[1, 0]),
        pltpu.make_async_copy(v_hbm.at[pl.ds(0, PIECE)], v_all.at[1, NEAR], v_recv.at[1, 0]),
    ]
    again = [
        pltpu.make_async_copy(kept.at[0, NEAR], kept.at[1, FAR], sem.at[1, 1])
        for kept, sem in ((tables, t_recv), (k_all, k_recv), (v_all, v_recv))
    ]
    for wanted, copies in forward:

        @pl.when(wanted)
        def _():
            for copy in copies():
                copy.start()

    @pl.when(at_fold)
    def _():
        for copy in across:
            copy.start()

    for copy in loads:
        copy.wait()

    for half in range(2):
        for i in range(BLOCKS):
            for h in range(HEADS):
                rows = slice(half * PIECE + i * BLOCK, half * PIECE + (i + 1) * BLOCK)
                to = slice(i * TILE + h * BLOCK, i * TILE + (h + 1) * BLOCK)
                cols = slice(h * HEAD_SIZE, (h + 1) * HEAD_SIZE)
                q_cat[half, to, :] = q_in[rows, cols]
                g_cat[half, to, :] = g_in[rows, cols]

    key_row = lax.broadcasted_iota(jnp.int32, (BLOCK, TILE), 0)
    query_row = lax.broadcasted_iota(jnp.int32, (BLOCK, TILE), 1) % BLOCK
    causal = key_row <= query_row

    def key_pass(half, chunk):
        k_t[half, chunk] = k_all[half, chunk].T
        for i in range(BLOCKS):
            begun = [starts[half * BLOCKS + j] for j in range(BLOCKS)]
            q_i = q_cat[half, lanes_of(i), :]
            scores = []
            for j in span(chunk, i):
                x = last_dims(k_all[half, chunk, rows_of(j), :], q_i) * exp2_scaling
                if chunk == OWN:
                    count = functools.reduce(lambda a, b: a + b, begun[j + 1 : i + 1], jnp.int32(0))
                    since = jnp.full((1, BLOCK), count.astype(jnp.float32))
                else:
                    count = functools.reduce(lambda a, b: a + b, begun[: i + 1])
                    since = tables[half, chunk, j : j + 1, :] + count.astype(jnp.float32)
                    if chunk == FAR:
                        since = since + tables[half, NEAR, BLOCKS : BLOCKS + 1, :]
                if not (chunk == OWN and j == i):
                    bias = jnp.where(since > 0.5, MASKED, 0.0)
                    x = x + jnp.concatenate([bias, bias], axis=1)
                if chunk == OWN and j == i:
                    x = jnp.where(causal, x, MASKED)
                if chunk == FAR and j == i:
                    x = jnp.where(causal, MASKED, x)
                scores.append(x)
            top = functools.reduce(jnp.maximum, [jnp.max(x, axis=0, keepdims=True) for x in scores])
            total = jnp.zeros((1, TILE), jnp.float32)
            for j, x in zip(span(chunk, i), scores):
                e = jnp.exp2(x - top)
                total = total + jnp.sum(e, axis=0, keepdims=True)
                terms[half, chunk, rows_of(j), lanes_of(i)] = e
            stats[half, chunk, 0:1, lanes_of(i)] = top
            stats[half, chunk, 1:2, lanes_of(i)] = total

    def value_pass(half, chunk):
        for i in range(BLOCKS):
            g_i = g_cat[half, lanes_of(i), :]
            dotted = jnp.zeros((1, TILE), jnp.float32)
            for j in span(chunk, i):
                w = last_dims(v_all[half, chunk, rows_of(j), :], g_i)
                dotted = dotted + jnp.sum(terms[half, chunk, rows_of(j), lanes_of(i)] * w, axis=0, keepdims=True)
                dweights[half, chunk, rows_of(j), lanes_of(i)] = w
            stats[half, chunk, 2:3, lanes_of(i)] = dotted

    def first_pass(half, chunk):
        key_pass(half, chunk)
        value_pass(half, chunk)

    def merge(half):
        tops = [stats[half, c, 0:1, :] for c in range(3)]
        top = functools.reduce(jnp.maximum, tops)
        ratios = [jnp.exp2(t - top) for t in tops]
        total = sum(stats[half, c, 1:2, :] * ratios[c] for c in range(3))
        dotted = sum(stats[half, c, 2:3, :] * ratios[c] for c in range(3))
        inverse = 1.0 / total
        for c in range(3):
            stats[half, c, 3:4, :] = ratios[c] * inverse
        stats[half, OWN, 4:5, :] = dotted * inverse

    def second_pass(half, chunk, blocks=range(BLOCKS)):
        for j in blocks:
            dk = jnp.zeros((BLOCK, HEAD_SIZE), jnp.float32)
            dv = jnp.zeros((BLOCK, HEAD_SIZE), jnp.float32)
            for i in range(BLOCKS):
                if j not in span(chunk, i):
                    continue
                p = terms[half, chunk, rows_of(j), lanes_of(i)] * stats[half, chunk, 3:4, lanes_of(i)]
                d = p * (dweights[half, chunk, rows_of(j), lanes_of(i)] - stats[half, OWN, 4:5, lanes_of(i)])
                d = d.astype(jnp.bfloat16)
                dscores[half, chunk, rows_of(j), lanes_of(i)] = d
                dk = dk + jnp.dot(d, q_cat[half, lanes_of(i), :], preferred_element_type=jnp.float32)
                dv = dv + jnp.dot(
                    p.astype(jnp.bfloat16), g_cat[half, lanes_of(i), :], preferred_element_type=jnp.float32)
            both = jnp.concatenate([dk * query_scaling, dv], axis=1)
            if chunk == OWN:
                grads_own[half, rows_of(j), :] = both
            else:
                grads_out[half, chunk - 1, rows_of(j), :] = both.astype(jnp.bfloat16)

    def query_pass(half):
        for i in range(BLOCKS):
            total = jnp.zeros((HEAD_SIZE, TILE), jnp.float32)
            for c in range(3):
                js = span(c, i)
                keys = slice(js[0] * BLOCK, (js[-1] + 1) * BLOCK)
                total = total + jnp.dot(
                    k_t[half, c, :, keys], dscores[half, c, keys, lanes_of(i)], preferred_element_type=jnp.float32)
            turned = (total * query_scaling).T.astype(jnp.bfloat16)
            rows = pl.ds(half * PIECE + i * BLOCK, BLOCK)
            for h in range(HEADS):
                dq_out[rows, h * HEAD_SIZE : (h + 1) * HEAD_SIZE] = turned[h * BLOCK : (h + 1) * BLOCK, :]

    def await_piece(half, slot):
        return [
            pltpu.make_async_copy(*refs)
            for refs in zip(own_refs(0), at(pieces, half, slot), at(recvs, half, slot - 1))
        ]

    def await_near(half):
        for part in range(2):
            rows = part_rows(part)
            pltpu.make_async_copy(
                grads_out.at[0, 0, rows], grads_in.at[half, NEAR, rows], g_recv.at[2 * part + half, 0]).wait()

    def await_grads(half, slot):
        pltpu.make_async_copy(grads_out.at[0, 0], grads_in.at[half, slot], g_recv.at[half, slot - 1]).wait()

    def part_rows(part):
        return pl.ds(LARGER * BLOCK, PIECE - LARGER * BLOCK) if part else pl.ds(0, LARGER * BLOCK)

    def near_grads(half, part):
        rows = part_rows(part)
        return pltpu.make_async_remote_copy(
            grads_out.at[half, NEAR - 1, rows], grads_in.at[half, NEAR, rows], g_send.at[2 * part + half, 0],
            g_recv.at[2 * part + half, 0], device_id=(jnp.where(half == 0, s - 1, s + 1), head), device_id_type=MESH)

    def far_grads(half):
        there = jnp.where(half == 0, s - 2, beyond)
        return pass_grads(half, FAR, there, jnp.where((half == 0) | folded, 0, 1))

    def near_wanted(half):
        return jnp.where(half == 0, s >= 1, s < n - 1)

    def far_wanted(half):
        return jnp.where(half == 0, s >= 2, s < n - 1)

    def near_aside():
        return pltpu.make_async_remote_copy(
            grads_out.at[0, NEAR - 1, part_rows(1)], g_hop, g_send.at[2, 1], g_recv.at[2, 1],
            device_id=(n - 1, head), device_id_type=MESH)

    def near_onward():
        return pltpu.make_async_remote_copy(
            g_hop, grads_in.at[0, NEAR, part_rows(1)], g_send.at[3, 1], g_recv.at[2, 0],
            device_id=(n - 3, head), device_id_type=MESH)

    before_fold = s == n - 2

    def home(part):
        rows = part_rows(part)
        return pltpu.make_async_copy(
            grads_out.at[1, NEAR - 1, rows], grads_in.at[0, NEAR, rows], g_recv.at[2 * part, 0])

    for half in range(2):
        first_pass(half, OWN)

    def earlier_pieces(turn, carry):
        half = jnp.where(turn == 0, first, 1 - first)

        @pl.when((half == 1) | (s >= 2))
        def _():
            for which, (awaited, copy) in enumerate(zip(await_piece(half, FAR), relay())):
                awaited.wait()
                able = relays & ~at_fold if which == 1 else relays

                @pl.when(able & (turn == 0))
                def _():
                    copy.start()

        @pl.when((s == n - 4) & (turn == 0))
        def _():
            pltpu.make_async_copy(own_refs(0)[1], k_hop, k_recv.at[2, 0]).wait()
            onward().start()

        @pl.when((half == 1) | (s >= 1))
        def _():
            await_piece(half, NEAR)[0].wait()

        first_pass(half, FAR)

        @pl.when((half == 1) | (s >= 1))
        def _():
            await_piece(half, NEAR)[1].wait()

        key_pass(half, NEAR)

        @pl.when((half == 1) | (s >= 1))
        def _():
            await_piece(half, NEAR)[2].wait()

        @pl.when(at_fold & (turn == 0))
        def _():
            for copy in again:
                copy.start()

        value_pass(half, NEAR)
        merge(half)
        def near_block():
            for part in range(2):
                second_pass(half, NEAR, range(LARGER, BLOCKS) if part else range(LARGER))

                through = before_fold & (half == 0) & (part == 1)

                @pl.when(near_wanted(half) & ~(at_fold & (half == 0)) & ~through)
                def _():
                    near_grads(half, part).start()

                @pl.when(through)
                def _():
                    near_aside().start()
                    far_grads(1).start()

                @pl.when(at_fold & (half == 1))
                def _():
                    home(part).start()

        def far_block():
            second_pass(half, FAR)

            @pl.when(far_wanted(half) & ~(before_fold & (half == 1)))
            def _():
                far_grads(half).start()

        near_block()
        far_block()

        @pl.when(at_fold & (half == 1))
        def _():
            both = grads_out[0, NEAR - 1].astype(jnp.float32) + grads_out[1, FAR - 1].astype(jnp.float32)
            grads_out[0, NEAR - 1] = both.astype(jnp.bfloat16)
            for part in range(2):
                near_grads(0, part).start()

        return carry

    lax.fori_loop(0, 2, earlier_pieces, 0)

    for half in range(2):
        second_pass(half, OWN)
        query_pass(half)

    @pl.when(at_fold)
    def _():
        pltpu.make_async_copy(grads_out.at[0, 0, part_rows(1)], g_hop, g_recv.at[2, 1]).wait()
        near_onward().start()

    def total_grads(turn, carry):
        half = jnp.where(turn == 0, 1 - first, first)
        @pl.when((half == 0) | (s >= 1))
        def _():
            await_near(half)

        @pl.when(jnp.where(half == 0, s != n - 2, s >= 2))
        def _():
            await_grads(half, FAR)

        total = (
            grads_own[half]
            + grads_in[half, NEAR].astype(jnp.float32)
            + grads_in[half, FAR].astype(jnp.float32)
        ).astype(jnp.bfloat16)
        piece = pl.ds(pl.multiple_of(half * PIECE, PIECE), PIECE)
        dk_out[piece, :] = total[:, :HEAD_SIZE]
        dv_out[piece, :] = total[:, HEAD_SIZE:]
        return carry

    lax.fori_loop(0, 2, total_grads, 0)

    for wanted, copies in forward:

        @pl.when(wanted)
        def _():
            for copy in copies():
                copy.wait_send()

    for which, copy in enumerate(relay()):

        @pl.when(relays & ~at_fold if which == 1 else relays)
        def _():
            copy.wait_send()

    @pl.when(s == n - 4)
    def _():
        onward().wait_send()

    @pl.when(at_fold)
    def _():
        near_onward().wait_send()

    for half in range(2):

        @pl.when(near_wanted(half))
        def _():
            near_grads(half, 0).wait_send()

        through = before_fold & (half == 0)

        @pl.when(near_wanted(half) & ~through)
        def _():
            near_grads(half, 1).wait_send()

        @pl.when(through)
        def _():
            near_aside().wait_send()

        @pl.when(far_wanted(half))
        def _():
            far_grads(half).wait_send()


def store_kernel(dq_ref, dk_ref, dv_ref, dq_hbm, dk_hbm, dv_hbm, sems):
    copies = []
    for which, (made, to) in enumerate(((dq_ref, dq_hbm), (dk_ref, dk_hbm), (dv_ref, dv_hbm))):
        for half in range(2):
            piece = pl.ds(half * PIECE, PIECE)
            copies.append(pltpu.make_async_copy(made.at[piece], to.at[piece], sems.at[2 * which + half]))
    for copy in copies:
        copy.start()
    for copy in copies:
        copy.wait()


def on_device(queries, keys, values, grad_out, starts):
    n = lax.axis_size("seq")
    bf16, f32 = jnp.bfloat16, jnp.float32
    vmem, dma = pltpu.VMEM, pltpu.SemaphoreType.DMA
    anywhere = pl.BlockSpec(memory_space=pl.ANY)
    shapes = (
        jax.ShapeDtypeStruct(queries.shape, bf16),
        jax.ShapeDtypeStruct(keys.shape, bf16),
        jax.ShapeDtypeStruct(values.shape, bf16),
    )
    made = pl.pallas_call(
        functools.partial(kernel, n),
        out_shape=shapes,
        in_specs=[anywhere] * 4 + [pl.BlockSpec(memory_space=pltpu.SMEM)],
        out_specs=(pl.BlockSpec(memory_space=pltpu.VMEM),) * 3,
        scratch_shapes=[
            vmem((2 * PIECE, 2 * HEAD_SIZE), bf16),
            vmem((2 * PIECE, 2 * HEAD_SIZE), bf16),
            vmem((2, 3, PIECE, HEAD_SIZE), bf16),
            vmem((2, 3, PIECE, HEAD_SIZE), bf16),
            vmem((2, 3, HEAD_SIZE, PIECE), bf16),
            vmem((2, 8, BLOCK), f32),
            vmem((2, 3, 8, BLOCK), f32),
            vmem((PIECE, HEAD_SIZE), bf16),
            vmem((2, LANES, HEAD_SIZE), bf16),
            vmem((2, LANES, HEAD_SIZE), bf16),
            vmem((2, 3, PIECE, LANES), f32),
            vmem((2, 3, PIECE, LANES), f32),
            vmem((2, 3, PIECE, LANES), bf16),
            vmem((2, 3, 8, LANES), f32),
            vmem((2, 2, PIECE, 2 * HEAD_SIZE), bf16),
            vmem((2, 3, PIECE, 2 * HEAD_SIZE), bf16),
            vmem((2, PIECE, 2 * HEAD_SIZE), f32),
            vmem((PIECE - LARGER * BLOCK, 2 * HEAD_SIZE), bf16),
            dma((6,)),
        ]
        + [dma((3, 2))] * 6 + [dma((4, 2))] * 2,
        compiler_params=pltpu.CompilerParams(
            collective_id=0, has_side_effects=True, vmem_limit_bytes=48 << 20
        ),
    )(*(pltpu.with_memory_space_constraint(x, pltpu.HBM) for x in (queries, grad_out, keys, values, starts)))
    return pl.pallas_call(
        store_kernel,
        out_shape=shapes,
        in_specs=[anywhere] * 3,
        out_specs=(pl.BlockSpec(memory_space=pltpu.HBM),) * 3,
        scratch_shapes=[dma((6,))],
        compiler_params=pltpu.CompilerParams(vmem_limit_bytes=1 << 20),
    )(*made)


def solution(mesh):
    in_specs = (P("seq", "head"), P("seq", "head"), P("seq", "head"), P("seq", "head"), P("seq"))
    out_specs = (P("seq", "head"), P("seq", "head"), P("seq", "head"))
    return jax.shard_map(
        on_device, mesh=mesh, in_specs=in_specs, out_specs=out_specs, check_vma=False
    )
```
